32 devices in a mesh: dp: 8 (over y, x, core), ctx: 4 (over z).
Axes of the slice: x: 2, y: 2, z: 4, core: 2. Of those that a mesh axis runs over, the one named last changes fastest.
Arguments:
- inputs: bfloat16 [8, 1024, 2048], P('dp', 'ctx'), may hold values from -6 to 6
- lengths: int32 [8], P('dp'), may hold values from 512 to 1024, as said below
- norm_gain: bfloat16 [2048], replicated, may hold values from 0.5 to 1.5
- up_weight: bfloat16 [2048, 8192], P('dp'), may hold values from -0.125 to 0.125
- conv_weight: bfloat16 [4, 4096], replicated, may hold values from -3 to 3
- conv_bias: bfloat16 [4096], replicated, may hold values from -3 to 3
- qkv_weight: bfloat16 [3, 4, 4, 4, 256], replicated, may hold values from -3 to 3
- gate_weight: bfloat16 [8, 12288], replicated, may hold values from -0.109375 to 0.109375
- gate_bias: bfloat16 [8], replicated, may hold values from -1 to 8.5
- skip_weight: bfloat16 [4096], replicated, may hold values from 0.5 to 1.5
- outnorm_weight: bfloat16 [4096], replicated, may hold values from 0.5 to 1.5
- down_weight: bfloat16 [4096, 2048], P('dp'), may hold values from -0.09375 to 0.09375
- grad_out: bfloat16 [8, 1024, 2048], P('dp', 'ctx'), may hold values from -6 to 6
Outputs:
- outputs: bfloat16 [8, 1024, 2048], P('dp', 'ctx')
- grad_inputs: float32 [8, 1024, 2048], P('dp', 'ctx')
- grad_norm_gain: float32 [2048], replicated
- grad_up_weight: float32 [2048, 8192], P('dp')
- grad_conv_weight: float32 [4, 4096], replicated
- grad_conv_bias: float32 [4096], replicated
- grad_qkv_weight: float32 [3, 4, 4, 4, 256], replicated
- grad_gate_weight: float32 [8, 12288], replicated
- grad_gate_bias: float32 [8], replicated
- grad_skip_weight: float32 [4096], replicated
- grad_outnorm_weight: float32 [4096], replicated
- grad_down_weight: float32 [4096, 2048], P('dp')
The draws below stay inside these ranges and needn't reach their ends.
Inputs may be any that keep to these rules, and one draw needn't show every extreme that they name: `lengths`: each entry counts the real tokens of a sequence from its start; one sequence has exactly 1024, another exactly 512.
All inputs are finite; a program needn't handle non-finite values.
Results may differ from the reference program's by a relative error of at most 0.04.
Values may be sent and summed in bfloat16 or wider, within the bound.
No kernel may reach another device: no remote copies, remote signals or barrier semaphores. Data moves between devices by JAX's collectives and lax.ppermute only.
A program may use at most 448 MiB of HBM per device.

```python
from functools import partial
import jax
import jax.numpy as jnp
from jax import lax

D = 2048
INNER = 4096
HEADS = 4
KSIZE = 4
QB = 4
LEN = 1024
SEQ_DEV = 256
QJ = 256
BATCH = 8
N_CTX = 4


def draw_lengths(key, part):
    first, second, third = jax.random.split(jax.random.fold_in(key, 11), 3)
    values = jax.random.randint(first, (BATCH,), LEN // 2, LEN + 1)
    full_slot = jax.random.randint(second, (), 0, BATCH)
    half_slot = (full_slot + jax.random.randint(third, (), 1, BATCH)) % BATCH
    slots = jnp.arange(BATCH)
    values = jnp.where(slots == full_slot, LEN, values)
    values = jnp.where(slots == half_slot, LEN // 2, values)
    return values.astype(jnp.int32)


def draw_gate_bias(key, part):
    first, second = jax.random.split(jax.random.fold_in(key, 23), 2)
    inputs_part = jax.random.uniform(first, (HEADS,), jnp.float32, -1.0, 1.0)
    forget_part = jax.random.uniform(second, (HEADS,), jnp.float32, 3.4, 8.0)
    return jnp.concatenate([inputs_part, forget_part]).astype(jnp.bfloat16)


def level_of(rng, extent, cuts, smallest, high):
    factor_of, own = 1.0, jax.random.fold_in(rng, 6)
    for axis_at, shards_of in cuts:
        draws = jnp.exp(jax.random.uniform(jax.random.fold_in(own, axis_at), (shards_of,), jnp.float32, smallest / len(cuts), high / len(cuts)))
        factor_of = factor_of * jnp.repeat(draws, extent[axis_at] // shards_of).reshape([-1 if axis == axis_at else 1 for axis in range(len(extent))])
    return factor_of


def normal_values(stream_key, extent, width, bound, cuts=(), held_as=jnp.bfloat16):
    array = jax.random.normal(stream_key, extent, jnp.float32) * width
    if len(cuts) > 0:
        array = level_of(stream_key, extent, cuts, -0.22, 0.18) * array
    return jnp.clip(array, min=-bound, max=bound).astype(held_as)


def setup_inputs(seed: int = 0) -> dict:
    key_list = jax.random.split(jax.random.key(seed), 14)
    inputs = normal_values(key_list[0], (BATCH, LEN, D), 1.0, 6.0, ((0, 8), (1, 4)))
    lengths = draw_lengths(jax.random.fold_in(key_list[13], 71), 0)
    norm_gain = jnp.clip(1.0 + 0.1 * jax.random.normal(key_list[2], (D,), jnp.float32), 0.5, 1.5).astype(jnp.bfloat16)
    up_weight = normal_values(key_list[3], (D, 2 * INNER), D ** -0.5, 0.125, ((0, 8),))
    conv_weight = normal_values(key_list[4], (KSIZE, INNER), KSIZE ** -0.5, 3.0)
    conv_bias = normal_values(key_list[5], (INNER,), 0.5, 3.0)
    qkv_weight = normal_values(key_list[6], (3, HEADS, QB, QB, QJ), QB ** -0.5, 3.0)
    gate_weight = normal_values(key_list[7], (2 * HEADS, 3 * INNER), (3 * INNER // 4) ** -0.5, 0.109375)
    gate_bias = draw_gate_bias(jax.random.fold_in(key_list[13], 71), 0)
    skip_weight = jnp.clip(jax.random.uniform(key_list[9], (INNER,), jnp.float32, 0.5, 1.5), 0.5, 1.5).astype(jnp.bfloat16)
    outnorm_weight = jnp.clip(jax.random.uniform(key_list[10], (INNER,), jnp.float32, 0.5, 1.5), 0.5, 1.5).astype(jnp.bfloat16)
    down_weight = normal_values(key_list[11], (INNER, D), INNER ** -0.5, 0.09375, ((0, 8),))
    grad_out = normal_values(key_list[12], (BATCH, LEN, D), 1.0, 6.0, ((0, 8), (1, 4)))
    return dict(inputs=inputs, lengths=lengths, norm_gain=norm_gain, up_weight=up_weight, conv_weight=conv_weight, conv_bias=conv_bias, qkv_weight=qkv_weight, gate_weight=gate_weight, gate_bias=gate_bias, skip_weight=skip_weight, outnorm_weight=outnorm_weight, down_weight=down_weight, grad_out=grad_out)


@jax.custom_vjp
def low(v):
    return lax.optimization_barrier(v.astype(jnp.bfloat16)).astype(jnp.float32)

@jax.custom_vjp
def low_back(v):
    return v

def low_keep(v):
    return (low(v), None)

def low_pass(kept, grad):
    return (grad,)

def back_keep(v):
    return (v, None)

def back_low(kept, grad):
    return (low(grad),)
low.defvjp(low_keep, low_pass)
low_back.defvjp(back_keep, back_low)
highest = lax.Precision.HIGHEST
epsilon = 1e-05

def layer_norm_low(rows_in, gain_row):
    centred = rows_in - lax.optimization_barrier(jnp.mean(rows_in, axis=-1, keepdims=True))
    spread = lax.optimization_barrier(jnp.mean(centred * centred, axis=-1, keepdims=True))
    return low(centred * lax.rsqrt(spread + epsilon) * gain_row)

def headwise(values_in, blocks_in):
    row_count, width_all = values_in.shape
    head_count, block_size, block_out, block_count = blocks_in.shape
    grouped = values_in.reshape(row_count, head_count, block_size, block_count)
    mixed_rows = jnp.einsum('thij,hioj->thoj', grouped, blocks_in, precision=highest)
    return mixed_rows.reshape(row_count, width_all)

def split_heads(rows_in, head_count):
    return rows_in.reshape(rows_in.shape[0], head_count, -1).transpose(1, 0, 2)

def mid_section(mixer_in, rim_rows, conv_taps, conv_shift, qkv_blocks, gate_matrix, gate_offset):
    row_count, width_all = mixer_in.shape
    kernel_size = conv_taps.shape[0]
    head_count = qkv_blocks.shape[1]
    padded_in = jnp.concatenate([rim_rows, mixer_in], axis=0)
    conv_pre = conv_shift[None, :] + conv_taps[0][None, :] * padded_in[0:row_count]
    for tap_index in range(1, kernel_size):
        conv_pre = conv_pre + conv_taps[tap_index][None, :] * padded_in[tap_index:tap_index + row_count]
    conv_out = jax.nn.silu(conv_pre)
    key_scale = (width_all // head_count) ** (-0.5)
    queries = low(headwise(conv_out, qkv_blocks[0]))
    key_rows = low(headwise(conv_out, qkv_blocks[1]) * key_scale)
    value_rows = low(headwise(mixer_in, qkv_blocks[2]))
    joined = jnp.concatenate([queries, key_rows, value_rows], axis=1)
    gate_pre = jnp.dot(joined, gate_matrix.T, precision=highest) + gate_offset[None, :]
    return (queries, key_rows, value_rows, gate_pre[:, :head_count], jax.nn.log_sigmoid(gate_pre[:, head_count:]), conv_out)

def cell_out(queries, key_rows, value_rows, in_gate, log_forget, state_in):
    row_count, width_all = queries.shape
    head_count = state_in.shape[0]
    query_heads = split_heads(queries, head_count)
    key_heads = split_heads(key_rows, head_count)
    value_heads = split_heads(value_rows, head_count)
    decay_sum = jnp.cumsum(log_forget, axis=0).T
    gate_row = in_gate.T
    causal = jnp.arange(row_count)[:, None] >= jnp.arange(row_count)[None, :]
    exponent = decay_sum[:, :, None] - decay_sum[:, None, :] + gate_row[:, None, :]
    weights = jnp.where(causal[None], jnp.exp(jnp.where(causal[None], exponent, 0.0)), 0.0)
    scores = low_back(jnp.einsum('htk,hsk->hts', query_heads, key_heads, precision=highest))
    mix_weights = low(weights * scores)
    within = jnp.einsum('hts,hsd->htd', mix_weights, value_heads, precision=highest)
    carried = jnp.einsum('htk,hkd->htd', query_heads, low(state_in), precision=highest)
    numerator = low_back(within + jnp.exp(decay_sum)[:, :, None] * carried)
    return numerator.transpose(1, 0, 2).reshape(row_count, width_all)

def summary(key_rows, value_rows, in_gate, log_forget):
    head_count = in_gate.shape[1]
    decay_sum = jnp.cumsum(log_forget, axis=0)
    span_decay = decay_sum[-1]
    weights = jnp.exp(span_decay[None, :] - decay_sum + in_gate)
    weighted = low(split_heads(key_rows, head_count) * weights.T[:, :, None])
    state_part = low_back(jnp.einsum('htk,htd->hkd', weighted, split_heads(value_rows, head_count), precision=highest))
    return (state_part, span_decay)

def tail_section(numerator, conv_out, gate_in, outnorm_scale, skip_scale, head_count):
    row_count, width_all = numerator.shape
    grouped = numerator.reshape(row_count, head_count, -1)
    centred = grouped - lax.optimization_barrier(jnp.mean(grouped, axis=-1, keepdims=True))
    spread = lax.optimization_barrier(jnp.mean(centred * centred, axis=-1, keepdims=True))
    normed = (centred * lax.rsqrt(spread + epsilon)).reshape(row_count, width_all) * outnorm_scale
    return low((normed + skip_scale * conv_out) * jax.nn.silu(gate_in))

def forward(lengths, input_rows, norm_scale, up_matrix, conv_taps, conv_shift, qkv_blocks, gate_matrix, gate_offset, skip_scale, outnorm_scale, down_matrix):
    inner_width = conv_taps.shape[1]
    head_count = qkv_blocks.shape[1]
    kernel_size = conv_taps.shape[0]
    seq_total = input_rows.shape[1]
    positions = jnp.arange(seq_total)
    head_dim = inner_width // head_count

    def one_sequence(unused_carry, seq_pair):
        rows_in, length_now = seq_pair
        normed = layer_norm_low(rows_in, norm_scale)
        upward = low_back(jnp.dot(normed, up_matrix, precision=highest))
        mixer_in = low(upward[:, :inner_width])
        gate_in = upward[:, inner_width:]
        rim_rows = jnp.zeros((kernel_size - 1, inner_width), jnp.float32)
        queries, key_rows, value_rows, in_gate, log_forget, conv_out = mid_section(mixer_in, rim_rows, conv_taps, conv_shift, qkv_blocks, gate_matrix, gate_offset)

        def by_spans(values_in):
            return values_in.reshape((N_CTX, SEQ_DEV) + values_in.shape[1:])

        def span_step(state_in, pieces):
            numerator = cell_out(pieces[0], pieces[1], pieces[2], pieces[3], pieces[4], state_in)
            state_part, span_decay = summary(pieces[1], pieces[2], pieces[3], pieces[4])
            return (jnp.exp(span_decay)[:, None, None] * state_in + state_part, numerator)
        start_state = jnp.zeros((head_count, head_dim, head_dim), jnp.float32)
        span_inputs = (by_spans(queries), by_spans(key_rows), by_spans(value_rows), by_spans(in_gate), by_spans(log_forget))
        final_state, numerators = lax.scan(jax.checkpoint(span_step), start_state, span_inputs)
        numerator = numerators.reshape(seq_total, inner_width)
        hidden_state = tail_section(numerator, conv_out, gate_in, outnorm_scale, skip_scale, head_count)
        branch = low_back(jnp.dot(hidden_state, down_matrix, precision=highest))
        live_rows = (positions < length_now).astype(jnp.float32)[:, None]
        return (unused_carry, live_rows * (rows_in + branch))
    ignored, outputs = lax.scan(jax.checkpoint(one_sequence), jnp.zeros((), jnp.float32), (input_rows, lengths))
    return outputs

def reference(inputs, lengths, norm_gain, up_weight, conv_weight, conv_bias, qkv_weight, gate_weight, gate_bias, skip_weight, outnorm_weight, down_weight, grad_out):
    floats = tuple((array_in.astype(jnp.float32) for array_in in (inputs, norm_gain, up_weight, conv_weight, conv_bias, qkv_weight, gate_weight, gate_bias, skip_weight, outnorm_weight, down_weight)))
    outputs, pullback = jax.vjp(partial(forward, lengths), *floats)
    gradients = pullback(grad_out.astype(jnp.float32))
    return (outputs.astype(jnp.bfloat16), gradients[0], gradients[1], gradients[2], gradients[3], gradients[4], gradients[5], gradients[6], gradients[7], gradients[8], gradients[9], gradients[10])
```

```python
from functools import partial

import jax
import jax.numpy as jnp
from jax import lax
from jax.experimental import pallas as pl
from jax.experimental.pallas import tpu as pltpu
from jax.sharding import PartitionSpec as P

epsilon = 1e-05
f32 = jnp.float32
bf16 = jnp.bfloat16


def dot_nn(a, b):
    return lax.dot_general(a, b, (((1,), (0,)), ((), ())), preferred_element_type=f32)


def dot_nt(a, b):
    return lax.dot_general(a, b, (((1,), (1,)), ((), ())), preferred_element_type=f32)


def dot_tn(a, b):
    return lax.dot_general(a, b, (((0,), (0,)), ((), ())), preferred_element_type=f32)


def normalize(rows):
    centred = rows - jnp.mean(rows, axis=-1, keepdims=True)
    scale = lax.rsqrt(jnp.mean(centred * centred, axis=-1, keepdims=True) + epsilon)
    return centred * scale, scale


def normalize_back(grad, normed, scale):
    return scale * (
        grad
        - jnp.mean(grad, axis=-1, keepdims=True)
        - normed * jnp.mean(grad * normed, axis=-1, keepdims=True)
    )


def silu_parts(x):
    sig = jax.nn.sigmoid(x)
    return sig, x * sig


def fold8(x):
    rows = x.shape[0]
    out = x[0:8]
    for at in range(8, rows, 8):
        out = out + x[at : at + 8]
    return out


def whole(shape):
    return pl.BlockSpec(shape, lambda *g: (0,) * len(shape), pipeline_mode=pl.Buffered(1))


def call(kernel, place, grid, in_specs, out_specs, out_shape, scratch, estimate, name, *args):
    return pl.pallas_call(
        kernel,
        grid_spec=pltpu.PrefetchScalarGridSpec(
            num_scalar_prefetch=1,
            grid=(grid,),
            in_specs=in_specs,
            out_specs=out_specs,
            scratch_shapes=scratch,
        ),
        out_shape=out_shape,
        compiler_params=kernel_params(),
        cost_estimate=estimate,
        name=name,
    )(place, *args)


def kernel_params(limit=48):
    return pltpu.CompilerParams(
        dimension_semantics=("arbitrary",), vmem_limit_bytes=limit * 1024 * 1024
    )


def cost(flops, moved, transcendentals=0):
    return pl.CostEstimate(
        flops=int(flops), bytes_accessed=int(moved), transcendentals=int(transcendentals)
    )


def row_chunks(rows, size, body, together=1):
    def step(n, carry):
        for m in range(together):
            body(pl.multiple_of((n * together + m) * size, size))
        return carry

    lax.fori_loop(0, rows // (size * together), step, 0)


def front_kernel(
    key_scale, at_ref, mix_ref, prev_ref, taps_ref, shift_ref, maps_ref, gates_ref,
    pre_ref, q_ref, k_ref, v_ref, part_ref, pad_ref,
):
    rows, width = mix_ref.shape
    taps = taps_ref.shape[0]
    lanes = maps_ref.shape[1]
    block = width // lanes
    first = pl.program_id(0) == 0
    before = prev_ref[...].astype(f32)[prev_ref.shape[0] - 8 :]
    pad_ref[0:8, :] = jnp.where(first, jnp.zeros_like(before), before)
    pad_ref[8 : 8 + rows, :] = mix_ref[...].astype(f32)

    def chunk(at):
        size = 16
        conv, mixed = [], []
        for i in range(block):
            cols = slice(i * lanes, (i + 1) * lanes)
            x = pad_ref[pl.ds(at, size + 8), cols]
            pre = shift_ref[:, cols]
            for j in range(taps):
                lag = taps - 1 - j
                pre = pre + taps_ref[j : j + 1, cols] * x[8 - lag : 8 - lag + size]
            pre_ref[pl.ds(at, size), cols] = pre
            conv.append(silu_parts(pre)[1])
            mixed.append(x[8:])

        def mapped(m, parts, o):
            out = parts[0] * maps_ref[m * block * block + o : m * block * block + o + 1, :]
            for i in range(1, block):
                r = (m * block + i) * block + o
                out = out + parts[i] * maps_ref[r : r + 1, :]
            return out

        for o in range(block):
            cols = slice(o * lanes, (o + 1) * lanes)
            q_ref[pl.ds(at, size), cols] = mapped(0, conv, o).astype(bf16)
            k_ref[pl.ds(at, size), cols] = (mapped(1, conv, o) * key_scale).astype(bf16)
            v_ref[pl.ds(at, size), cols] = mapped(2, mixed, o).astype(bf16)

    row_chunks(rows, 16, chunk)
    part_ref[...] = (
        dot_nt(gates_ref[0], q_ref[...])
        + dot_nt(gates_ref[1], k_ref[...])
        + dot_nt(gates_ref[2], v_ref[...])
    )


def front(place, mixer, conv_taps, conv_shift, maps, gate_rows, key_scale, span):
    total, width = mixer.shape
    count = total // span
    step = span // 16

    def own(i, at):
        return (lax.rem(i + count - at[0], count), 0)

    def ahead(i, at):
        return (lax.rem(i + count - 1 - at[0] + count, count) * step + step - 1, 0)

    tile = pl.BlockSpec((span, width), lambda i, at: (i, 0))
    gates_of = gate_rows.shape[1]
    return call(
        partial(front_kernel, key_scale),
        place,
        count,
        [
            pl.BlockSpec((span, width), own),
            pl.BlockSpec((16, width), ahead),
            whole(conv_taps.shape),
            whole(conv_shift.shape),
            whole(maps.shape),
            whole(gate_rows.shape),
        ],
        [tile, tile, tile, tile, pl.BlockSpec((gates_of, span), lambda i, at: (0, i))],
        [
            jax.ShapeDtypeStruct((total, width), f32),
            *[jax.ShapeDtypeStruct((total, width), bf16)] * 3,
            jax.ShapeDtypeStruct((gates_of, total), f32),
        ],
        [pltpu.VMEM((span + 8, width), f32)],
        cost(6e9, 12 * total * width, total * width),
        "front",
        mixer, mixer, conv_taps, conv_shift, maps, gate_rows,
    )


def gates_kernel(span, share, head_ref, *refs):
    parts, bias_ref, out_ref = refs[:-2], refs[-2], refs[-1]
    pre = parts[0][...]
    for p in parts[1:]:
        pre = pre + p[...]
    if share != 1.0:
        pre = pre * share
    pre = pre + bias_ref[...]
    rows, total = pre.shape
    head = head_ref[0]
    at = lax.broadcasted_iota(jnp.int32, pre.shape, 0)
    lane = lax.broadcasted_iota(jnp.int32, (8, total), 1)
    in_gate = jnp.sum(jnp.where(at == head, pre, 0.0), axis=0, keepdims=True)
    forget = jnp.sum(jnp.where(at == head + rows // 2, pre, 0.0), axis=0, keepdims=True)
    forget = jnp.broadcast_to(forget, (8, total))
    log_forget = jnp.minimum(forget, 0.0) - jnp.log1p(jnp.exp(-jnp.abs(forget)))
    place = lane % span
    running = log_forget
    by = 1
    while by < span:
        running = running + jnp.where(place >= by, pltpu.roll(running, by, 1), 0.0)
        by *= 2
    whole_sum = jnp.where(place == span - 1, running, 0.0)
    by = 1
    while by < span:
        whole_sum = whole_sum + pltpu.roll(whole_sum, total - by, 1) * jnp.where(
            place < span - by, 1.0, 0.0
        )
        by *= 2
    out_ref[0:1, :] = in_gate
    out_ref[1:2, :] = running[0:1]
    out_ref[2:3, :] = whole_sum[0:1]
    out_ref[3:4, :] = jax.nn.sigmoid(-forget)[0:1]
    out_ref[4:8, :] = jnp.zeros((4, total), f32)


def gates(head, parts, bias, span, share):
    rows, total = parts[0].shape
    full = pl.BlockSpec((rows, total), lambda i, s: (0, 0))
    return pl.pallas_call(
        partial(gates_kernel, span, share),
        grid_spec=pltpu.PrefetchScalarGridSpec(
            num_scalar_prefetch=1,
            grid=(1,),
            in_specs=[full] * len(parts) + [pl.BlockSpec((rows, 1), lambda i, s: (0, 0))],
            out_specs=pl.BlockSpec((8, total), lambda i, s: (0, 0)),
        ),
        out_shape=jax.ShapeDtypeStruct((8, total), f32),
        name="gates",
    )(head.reshape(1).astype(jnp.int32), *parts, bias)


def column_of(row):
    n = row.shape[1]
    eye = lax.broadcasted_iota(jnp.int32, (n, n), 0) == lax.broadcasted_iota(jnp.int32, (n, n), 1)
    return jnp.sum(jnp.where(eye, jnp.broadcast_to(row, (n, n)), 0.0), axis=1, keepdims=True)


def row_of(column):
    n = column.shape[0]
    eye = lax.broadcasted_iota(jnp.int32, (n, n), 0) == lax.broadcasted_iota(jnp.int32, (n, n), 1)
    return jnp.sum(jnp.where(eye, jnp.broadcast_to(column, (n, n)), 0.0), axis=0, keepdims=True)


def tile_weights(gate_ref, column, reach, lanes, n, causal):
    row = gate_ref[0:1, lanes] - gate_ref[1:2, lanes] + reach
    exponent = column + row
    if not causal:
        return jnp.exp(exponent)
    keep = lax.broadcasted_iota(jnp.int32, (n, n), 0) >= lax.broadcasted_iota(jnp.int32, (n, n), 1)
    return jnp.where(keep, jnp.exp(jnp.where(keep, exponent, 0.0)), 0.0)


def cell_kernel(
    at_ref, gate_ref, q_ref, k_ref, v_ref, pre_ref, gin_ref, skip_ref, og_ref,
    mix_ref, num_ref, hid_ref,
):
    n, width = q_ref.shape
    tb = pl.program_id(0)
    here = pl.ds(pl.multiple_of(tb * n, n), n)
    column = column_of(gate_ref[1:2, here])

    def one(sb, reach, causal):
        lanes = pl.ds(pl.multiple_of(sb * n, n), n)
        w = tile_weights(gate_ref, column, reach, lanes, n, causal)
        mix = (w * dot_nt(q_ref[...], k_ref[lanes, :])).astype(bf16)
        mix_ref[:, lanes] = mix
        return dot_nn(mix, v_ref[lanes, :])

    num_ref[...] = one(tb, jnp.zeros((1, n), f32), True)

    def earlier(step, reach):
        sb = tb - 1 - step
        reach = reach + gate_ref[2:3, pl.ds(pl.multiple_of(sb * n, n), n)]
        num_ref[...] += one(sb, reach, False)
        return reach

    lax.fori_loop(0, tb, earlier, jnp.zeros((1, n), f32))
    skip, og = skip_ref[...], og_ref[...]

    def chunk(at):
        rows = pl.ds(at, 16)
        hat, _ = normalize(num_ref[rows, :])
        conv = silu_parts(pre_ref[rows, :])[1]
        act = silu_parts(gin_ref[rows, :])[1]
        hid_ref[rows, :] = ((hat * og + skip * conv) * act).astype(bf16)

    row_chunks(n, 16, chunk, 4)


def cell(place, gate, q, k, v, pre, gate_in, skip, out_gain, span):
    total, width = q.shape
    count = total // span

    def own(i, at):
        return (lax.rem(i + count - at[0], count), 0)

    tile = pl.BlockSpec((span, width), lambda i, at: (i, 0))
    moved = pl.BlockSpec((span, width), own)
    full = whole((total, width))
    return call(
        cell_kernel,
        place,
        count,
        [whole(gate.shape), tile, full, full, tile, moved, whole(skip.shape), whole(out_gain.shape)],
        [pl.BlockSpec((span, total), lambda i, at: (i, 0)), tile, moved],
        [
            jax.ShapeDtypeStruct((total, total), bf16),
            jax.ShapeDtypeStruct((total, width), f32),
            jax.ShapeDtypeStruct((total, width), bf16),
        ],
        [],
        cost(2.5 * total * width * total, 20 * total * width, 3 * total * width),
        "cell",
        gate, q, k, v, pre, gate_in, skip, out_gain,
    )


def tail_back_kernel(
    at_ref, bg_ref, num_ref, pre_ref, gin_ref, down_ref, skip_ref, og_ref,
    ng_ref, gg_ref, ct_ref, sums_ref, hg_ref,
):
    hg_ref[...] = dot_nt(bg_ref[...], down_ref[...])

    @pl.when(pl.program_id(0) == 0)
    def _():
        sums_ref[...] = jnp.zeros_like(sums_ref)

    skip, og = skip_ref[...], og_ref[...]

    def chunk(at):
        rows = pl.ds(at, 16)
        hat, scale = normalize(num_ref[rows, :])
        conv = silu_parts(pre_ref[rows, :])[1]
        before = hat * og + skip * conv
        gin = gin_ref[rows, :]
        sig, act = silu_parts(gin)
        hg = hg_ref[rows, :]
        gg_ref[rows, :] = (hg * before * (sig * (1.0 + gin * (1.0 - sig)))).astype(bf16)
        bgrad = hg * act
        sums_ref[0:8, :] += fold8(bgrad * conv)
        sums_ref[8:16, :] += fold8(bgrad * hat)
        ct_ref[rows, :] = bgrad * skip
        ng_ref[rows, :] = normalize_back(bgrad * og, hat, scale).astype(bf16)

    row_chunks(hg_ref.shape[0], 16, chunk, 4)


def tail_back(place, bg, num, pre, gate_in, w_down, skip, out_gain, span):
    model = bg.shape[1]
    total, width = num.shape
    count = total // span

    def own(i, at):
        return (lax.rem(i + count - at[0], count), 0)

    tile = pl.BlockSpec((span, width), lambda i, at: (i, 0))
    moved = pl.BlockSpec((span, width), own)
    return call(
        tail_back_kernel,
        place,
        count,
        [
            pl.BlockSpec((span, model), own), tile, tile, moved,
            whole(w_down.shape), whole(skip.shape), whole(out_gain.shape),
        ],
        [tile, moved, tile, pl.BlockSpec((16, width), lambda i, at: (0, 0))],
        [
            jax.ShapeDtypeStruct((total, width), bf16),
            jax.ShapeDtypeStruct((total, width), bf16),
            jax.ShapeDtypeStruct((total, width), f32),
            jax.ShapeDtypeStruct((16, width), f32),
        ],
        [pltpu.VMEM((span, width), f32)],
        cost(2 * total * model * width, 24 * total * width, 2 * total * width),
        "tail_back",
        bg, num, pre, gate_in, w_down, skip, out_gain,
    )


def cell_back_kernel(
    gate_ref, q_ref, k_ref, v_ref, mix_ref, ng_ref,
    dq_ref, dk_ref, dv_ref, gout_ref, sums_ref,
):
    n, width = q_ref.shape
    total = k_ref.shape[0]
    tb = pl.program_id(0)
    here = pl.ds(pl.multiple_of(tb * n, n), n)
    column = column_of(gate_ref[1:2, here])

    @pl.when(tb == 0)
    def _():
        sums_ref[...] = jnp.zeros_like(sums_ref)

    def one(sb, reach, causal):
        lanes = pl.ds(pl.multiple_of(sb * n, n), n)
        w = tile_weights(gate_ref, column, reach, lanes, n, causal)
        mix = mix_ref[:, lanes]
        ng = ng_ref[...]
        mix_grad = dot_nt(ng, v_ref[lanes, :])
        exponent_grad = mix_grad * mix.astype(f32)
        scores_grad = (w * mix_grad).astype(bf16)
        sums_ref[0:1, lanes] += jnp.sum(exponent_grad, axis=0, keepdims=True)
        return (
            jnp.sum(exponent_grad, axis=1, keepdims=True),
            dot_nn(scores_grad, k_ref[lanes, :]),
            dot_tn(scores_grad, q_ref[...]),
            dot_tn(mix, ng),
            lanes,
        )

    by_row, dq, dk, dv, lanes = one(tb, jnp.zeros((1, n), f32), True)
    dq_ref[...] = dq
    dk_ref[lanes, :] = dk
    dv_ref[lanes, :] = dv

    def earlier(step, carry):
        reach, by_row = carry
        sb = tb - 1 - step
        reach = reach + gate_ref[2:3, pl.ds(pl.multiple_of(sb * n, n), n)]
        more, dq, dk, dv, lanes = one(sb, reach, False)
        dq_ref[...] += dq
        dk_ref[lanes, :] += dk
        dv_ref[lanes, :] += dv
        return reach, by_row + more

    _, by_row = lax.fori_loop(0, tb, earlier, (jnp.zeros((1, n), f32), by_row))
    sums_ref[1:2, here] = row_of(by_row)

    @pl.when(tb == pl.num_programs(0) - 1)
    def _():
        by_source = sums_ref[0:1, :]
        lane = lax.broadcasted_iota(jnp.int32, (8, total), 1)
        running = jnp.broadcast_to(sums_ref[1:2, :] - by_source, (8, total))
        by = 1
        while by < total:
            running = running + jnp.where(
                lane < total - by, pltpu.roll(running, total - by, 1), 0.0
            )
            by *= 2
        gout_ref[0:1, :] = by_source
        gout_ref[1:2, :] = running[0:1] * gate_ref[3:4, :]


def cell_back(gate, q, k, v, mix, num_grad, span):
    total, width = q.shape
    tile = pl.BlockSpec((span, width), lambda i: (i, 0))
    full = whole((total, width))
    return pl.pallas_call(
        cell_back_kernel,
        grid=(total // span,),
        in_specs=[
            whole(gate.shape), tile, full, full,
            pl.BlockSpec((span, total), lambda i: (i, 0)), tile,
        ],
        out_specs=[
            tile,
            pl.BlockSpec((total, width), lambda i: (0, 0)),
            pl.BlockSpec((total, width), lambda i: (0, 0)),
            pl.BlockSpec((2, total), lambda i: (0, 0)),
        ],
        out_shape=[
            *[jax.ShapeDtypeStruct((total, width), f32)] * 3,
            jax.ShapeDtypeStruct((2, total), f32),
        ],
        scratch_shapes=[pltpu.VMEM((8, total), f32)],
        compiler_params=kernel_params(),
        cost_estimate=cost(
            5 * total * total * width, 24 * total * width, total * total
        ),
        name="cell_back",
    )(gate, q, k, v, mix, num_grad)


def back_kernel(
    key_scale, heads, at_ref, dq_ref, dk_ref, dv_ref, q_ref, k_ref, v_ref, pre_ref, mix_ref, ct_ref,
    taps_ref, maps_ref, gates_ref, *refs,
):
    gate_parts, sums_ref = refs[:heads], refs[heads]
    mg_ref, pack_ref, tg_ref, wg_ref, grow_ref, gsum_ref, gb_ref, pg_ref, mv_ref = refs[heads + 1 :]
    rows, width = dq_ref.shape
    taps = taps_ref.shape[0]
    lanes = maps_ref.shape[1]
    block = width // lanes
    per_map = block * block

    @pl.when(pl.program_id(0) == 0)
    def _():
        tg_ref[...] = jnp.zeros_like(tg_ref)
        wg_ref[...] = jnp.zeros_like(wg_ref)
        grow_ref[...] = jnp.zeros_like(grow_ref)
        gsum_ref[...] = jnp.zeros_like(gsum_ref)
        pg_ref[rows : rows + 8, :] = jnp.zeros((8, width), f32)

    gg = jnp.concatenate([p[...] for p in gate_parts], axis=0)
    gsum_ref[...] += jnp.broadcast_to(jnp.sum(gg, axis=1, keepdims=True), gsum_ref.shape)
    high = gg.astype(bf16)
    low = (gg - high.astype(f32)).astype(bf16)
    for m, x_ref in enumerate((q_ref, k_ref, v_ref)):
        gb_ref[m] = dot_tn(high, gates_ref[m]) + dot_tn(low, gates_ref[m])
        grow_ref[m] += dot_nn(high, x_ref[...]) + dot_nn(low, x_ref[...])

    size = 16

    def chunk(at):
        here = pl.ds(at, size)

        def cols(i):
            return slice(i * lanes, (i + 1) * lanes)

        def weight(m, i, o):
            r = (m * block + i) * block + o
            return maps_ref[r : r + 1, :]

        pre = [pre_ref[here, cols(i)] for i in range(block)]
        parts = [silu_parts(p) for p in pre]
        conv_grad = [ct_ref[here, cols(i)] for i in range(block)]
        for m, (g_ref, scale) in enumerate(((dq_ref, None), (dk_ref, key_scale))):
            for o in range(block):
                g = g_ref[here, cols(o)] + gb_ref[m, here, cols(o)]
                if scale is not None:
                    g = g * scale
                for i in range(block):
                    conv_grad[i] = conv_grad[i] + g * weight(m, i, o)
                    wg_ref[m * per_map + i * block + o] += fold8(parts[i][1] * g)
        for i in range(block):
            sig = parts[i][0]
            pg_ref[here, cols(i)] = conv_grad[i] * (sig * (1.0 + pre[i] * (1.0 - sig)))
        mixed = [mix_ref[here, cols(i)].astype(f32) for i in range(block)]
        grads = [None] * block
        for o in range(block):
            g = dv_ref[here, cols(o)] + gb_ref[2, here, cols(o)]
            for i in range(block):
                term = g * weight(2, i, o)
                grads[i] = term if grads[i] is None else grads[i] + term
                wg_ref[2 * per_map + i * block + o] += fold8(mixed[i] * g)
        for i in range(block):
            mv_ref[here, cols(i)] = grads[i]

    row_chunks(rows, size, chunk)

    def second(at):
        here = pl.ds(at, size)
        for i in range(block):
            cols = slice(i * lanes, (i + 1) * lanes)
            x = pg_ref[pl.ds(at, size + 8), cols]
            m = mix_ref[here, cols].astype(f32)
            grad = mv_ref[here, cols]
            for j in range(taps):
                lead = taps - 1 - j
                moved = x[lead : lead + size]
                grad = grad + taps_ref[j : j + 1, cols] * moved
                tg_ref[j, :, cols] += fold8(moved * m)
            tg_ref[taps, :, cols] += fold8(x[0:size])
            mg_ref[here, cols] = grad.astype(bf16)

    row_chunks(rows, size, second)
    pg_ref[rows : rows + 8, :] = pg_ref[0:8, :]

    @pl.when(pl.program_id(0) == pl.num_programs(0) - 1)
    def _():
        pack_ref[...] = jnp.zeros_like(pack_ref)
        at = 0
        for j in range(taps + 1):
            pack_ref[at : at + 1, :] = jnp.sum(tg_ref[j], axis=0, keepdims=True)
            at += 1
        for r in range(3 * block):
            for o in range(block):
                pack_ref[at : at + 1, o * lanes : (o + 1) * lanes] = jnp.sum(
                    wg_ref[r * block + o], axis=0, keepdims=True
                )
            at += 1
        for m in range(3):
            pack_ref[at : at + 2 * heads, :] = grow_ref[m]
            at += 2 * heads
        for j in range(2):
            pack_ref[at : at + 1, :] = jnp.sum(sums_ref[8 * j : 8 * j + 8], axis=0, keepdims=True)
            at += 1
        sums = gsum_ref[...]
        diagonal = lax.broadcasted_iota(jnp.int32, sums.shape, 0) == lax.broadcasted_iota(
            jnp.int32, sums.shape, 1
        )
        pack_ref[at : at + 1, 0:128] = jnp.sum(
            jnp.where(diagonal, sums, 0.0), axis=0, keepdims=True
        )


def back(
    place, dq, dk, dv, gate_parts, q, k, v, pre, mixer, conv_tail, conv_taps, maps, gate_rows,
    tail_sums, key_scale, span, pack_rows,
):
    total, width = dq.shape
    count = total // span
    taps = conv_taps.shape[0]
    lanes = maps.shape[1]
    heads = len(gate_parts)

    def own(i, at):
        return (lax.rem(2 * count - 1 - i - at[0], count), 0)

    tile = pl.BlockSpec((span, width), lambda i, at: (count - 1 - i, 0))
    moved = pl.BlockSpec((span, width), own)
    return call(
        partial(back_kernel, key_scale, heads),
        place,
        count,
        [
            tile, tile, tile, tile, tile, tile, tile, moved, tile,
            whole(conv_taps.shape), whole(maps.shape), whole(gate_rows.shape),
            *[pl.BlockSpec((2, span), lambda i, at: (0, count - 1 - i))] * heads,
            whole(tail_sums.shape),
        ],
        [moved, pl.BlockSpec((pack_rows, width), lambda i, at: (0, 0))],
        [
            jax.ShapeDtypeStruct((total, width), bf16),
            jax.ShapeDtypeStruct((pack_rows, width), f32),
        ],
        [
            pltpu.VMEM((taps + 1, 8, width), f32),
            pltpu.VMEM((maps.shape[0], 8, lanes), f32),
            pltpu.VMEM(gate_rows.shape, f32),
            pltpu.VMEM((2 * heads, 128), f32),
            pltpu.VMEM((3, span, width), f32),
            pltpu.VMEM((span + 8, width), f32),
            pltpu.VMEM((span, width), f32),
        ],
        cost(12e9, 30 * total * width, 2 * total * width),
        "back",
        dq, dk, dv, q, k, v, pre, mixer, conv_tail, conv_taps, maps, gate_rows, *gate_parts,
        tail_sums,
    )


def assemble_kernel(count, at_ref, *refs):
    out_ref = refs[-1]
    inputs = refs[:-1]
    step = pl.program_id(0)
    halves = len(inputs) // (2 * count - 1)
    for half in range(halves):
        own, others = inputs[half * (2 * count - 1)], inputs[half * (2 * count - 1) + 1 : (half + 1) * (2 * count - 1)]
        at = half * count

        @pl.when(step == at)
        def _(ref=own):
            out_ref[...] = ref[...].astype(f32)

        for r in range(1, count):
            ahead, behind = others[2 * (r - 1)], others[2 * (count - r - 1) + 1]

            @pl.when((step == at + r) & (at_ref[0] + r < count))
            def _(ref=ahead):
                out_ref[...] = ref[...].astype(f32)

            @pl.when((step == at + r) & (at_ref[0] + r >= count))
            def _(ref=behind):
                out_ref[...] = ref[...].astype(f32)


def flat(own, hops):
    return [own] + [x for pair in hops for x in pair]


def assemble(place, own_mix, mix_hops, own_gate, gate_hops, copies):
    rows, width = own_mix.shape
    count = len(mix_hops) + 1
    heads = count // copies

    def out_map(i, at):
        half = i // count
        source = lax.rem(i - half * count + at[0], count)
        return (0, half * heads + source // copies)

    parts = flat(own_mix, mix_hops) + flat(own_gate, gate_hops)
    return call(
        partial(assemble_kernel, count),
        place,
        2 * count,
        [whole((rows, width))] * len(parts),
        pl.BlockSpec((rows, width), out_map),
        jax.ShapeDtypeStruct((rows, 2 * heads * width), f32),
        [],
        cost(0, 12 * count * rows * width),
        "assemble",
        *parts,
    )


def assemble_rows(place, own, hops):
    rows, width = own.shape
    count = len(hops) + 1
    parts = flat(own, hops)
    return call(
        partial(assemble_kernel, count),
        place,
        count,
        [whole((rows, width))] * len(parts),
        pl.BlockSpec((rows, width), lambda i, at: (lax.rem(i + at[0], count), 0)),
        jax.ShapeDtypeStruct((count * rows, width), f32),
        [],
        cost(0, 6 * count * rows * width),
        "assemble_rows",
        *parts,
    )


def mix_grads_kernel(x_ref, g_ref, w_ref, gain_ref, pack_ref, out_ref):
    rows = x_ref.shape[1]
    grad = dot_tn(x_ref[...], g_ref[...])
    out_ref[0, :rows, :] = grad.astype(bf16)
    gain = row_of(jnp.sum(grad * w_ref[...].astype(f32), axis=1, keepdims=True)) + gain_ref[0]
    width = out_ref.shape[2]
    extra = out_ref.shape[1] - rows
    pack = pack_ref[0]
    parts = [pack, jnp.concatenate([gain, jnp.zeros((1, width - rows), f32)], axis=1)]
    fill = extra - pack.shape[0] - 1
    if fill:
        parts.append(jnp.zeros((fill, width), f32))
    out_ref[0, rows:, :] = jnp.concatenate(parts, axis=0).astype(bf16)


def mix_grads(normed, mixer_grad, w_mix, gain_part, pack, dp):
    total, width = normed.shape
    cols = mixer_grad.shape[1]
    rows = width // dp
    pack = pack.reshape(dp, pack.shape[0] // dp, cols)
    extra = -(-(pack.shape[1] + 1) // 16) * 16
    return pl.pallas_call(
        mix_grads_kernel,
        grid=(dp,),
        in_specs=[
            pl.BlockSpec((total, rows), lambda i: (0, i)),
            whole(mixer_grad.shape),
            pl.BlockSpec((rows, cols), lambda i: (i, 0)),
            pl.BlockSpec((1, 1, rows), lambda i: (i, 0, 0)),
            pl.BlockSpec((1,) + pack.shape[1:], lambda i: (i, 0, 0)),
        ],
        out_specs=pl.BlockSpec((1, rows + extra, cols), lambda i: (i, 0, 0)),
        out_shape=jax.ShapeDtypeStruct((dp, rows + extra, cols), bf16),
        compiler_params=kernel_params(),
        cost_estimate=cost(2 * total * width * cols, 2 * (total * width + 3 * width * cols)),
        name="mix_grads",
    )(normed, mixer_grad, w_mix, gain_part.reshape(dp, 1, rows), pack)


def unpack_kernel(per, taps, heads, block, x_ref, gain_ref, norm_ref, convw_ref, convb_ref, maps_ref, gates_ref, bias_ref, skip_ref, og_ref):
    copies = x_ref.shape[0] // heads
    dp = x_ref.shape[1]
    width = x_ref.shape[3]
    lanes = width // block
    inner = heads * width
    rows = norm_ref.shape[1] // dp

    def row(h, r):
        return x_ref[h * copies, r // per, r % per : r % per + 1, :]

    for d in range(dp):
        total = x_ref[0, d, per : per + 1, 0:rows]
        for h in range(1, heads):
            total = total + x_ref[h * copies, d, per : per + 1, 0:rows]
        norm_ref[:, d * rows : (d + 1) * rows] = total / gain_ref[:, d * rows : (d + 1) * rows]
    for h in range(heads):
        cols = slice(h * width, (h + 1) * width)
        for j in range(taps):
            convw_ref[j : j + 1, cols] = row(h, j)
        convb_ref[:, cols] = row(h, taps)
        at = taps + 1
        for m in range(3):
            for i in range(block):
                values = row(h, at)
                for o in range(block):
                    maps_ref[m, h, i, o : o + 1, :] = values[:, o * lanes : (o + 1) * lanes]
                at += 1
        for m in range(3):
            for j in range(heads):
                for p in range(2):
                    g = p * heads + (h + j) % heads
                    start = m * inner + h * width
                    gates_ref[g : g + 1, start : start + width] = row(h, at)
                    at += 1
        skip_ref[:, cols] = row(h, at)
        og_ref[:, cols] = row(h, at + 1)
        if h == 0:
            bias_ref[...] = row(h, at + 2)[:, 0:128]


def unpack(small, gain, taps, heads, block):
    per, width = small.shape[2] - 1, small.shape[3]
    inner = heads * width
    shapes = [
        gain.shape, (taps, inner), (1, inner), (3, heads, block, block, width // block),
        (2 * heads, 3 * inner), (1, 128), (1, inner), (1, inner),
    ]
    return pl.pallas_call(
        partial(unpack_kernel, per, taps, heads, block),
        grid=(1,),
        in_specs=[whole(small.shape), whole(gain.shape)],
        out_specs=[pl.BlockSpec(x, lambda i, n=len(x): (0,) * n) for x in shapes],
        out_shape=[jax.ShapeDtypeStruct(x, f32) for x in shapes],
        compiler_params=kernel_params(),
        name="unpack",
    )(small, gain)


def after(x, *others):
    if isinstance(x, list):
        return list(lax.optimization_barrier((*x, *others))[: len(x)])
    return lax.optimization_barrier((x, *others))[0]


def fence(*values):
    return lax.optimization_barrier(values)


def pass_on(pair, axis, s):
    n = lax.axis_size(axis)
    return (
        lax.ppermute(pair[0], axis, [(i, i - 1) for i in range(1, n - s + 1)]),
        lax.ppermute(pair[1], axis, [(i, i + 1) for i in range(s - 1, n - 1)]),
    )


def in_turn(x, pairs, axis):
    n = lax.axis_size(axis)
    index = lax.axis_index(axis)
    parts = [x] + [
        jnp.where(index + r < n, pairs[r - 1][0], pairs[n - r - 1][1]) for r in range(1, n)
    ]
    return jnp.concatenate(parts, axis=0)


def scatter_on(blocks, moving, axis, s):
    n = lax.axis_size(axis)
    ahead, behind = blocks[n - s], blocks[s]
    if s > 1:
        ahead = (ahead.astype(f32) + moving[0].astype(f32)).astype(bf16)
        behind = (behind.astype(f32) + moving[1].astype(f32)).astype(bf16)
    return (
        lax.ppermute(ahead, axis, [(i, i + 1) for i in range(s)]),
        lax.ppermute(behind, axis, [(i, i - 1) for i in range(n - s, n)]),
    )


def scatter_sum(own, terms):
    total = own.astype(f32)
    for term in terms:
        total = total + term.astype(f32)
    return total


def spread(x, axis, offsets):
    n = lax.axis_size(axis)
    return [
        x if r == 0 else lax.ppermute(x, axis, [(i, (i - r) % n) for i in range(n)]) for r in offsets
    ]


def on_device(
    inputs,
    lengths,
    norm_gain,
    up_weight,
    conv_weight,
    conv_bias,
    qkv_weight,
    gate_weight,
    gate_bias,
    skip_weight,
    outnorm_weight,
    down_weight,
    grad_out,
):
    span = inputs.shape[1]
    width = inputs.shape[2]
    inner = conv_weight.shape[1]
    taps = conv_weight.shape[0]
    heads = qkv_weight.shape[1]
    block = qkv_weight.shape[2]
    head_dim = inner // heads
    dp = lax.axis_size("dp")
    ctx = lax.axis_size("ctx")
    copies = ctx // heads
    total = ctx * span
    ctx_index = lax.axis_index("ctx")
    place = ctx_index.reshape(1).astype(jnp.int32)
    head = ctx_index // copies
    share = 1.0 / copies

    def columns_of(w, start):
        return lax.dynamic_slice_in_dim(w, start, head_dim, axis=w.ndim - 1)

    def by_offset(x):
        return [x[r * span : (r + 1) * span] for r in range(ctx)]

    live = (ctx_index * span + jnp.arange(span) < lengths[0]).astype(f32)[:, None]
    x_own = inputs[0].astype(f32)
    out_grad = grad_out[0].astype(f32) * live
    gain = norm_gain.astype(f32)[None]
    own_hat, own_scale = normalize(x_own)
    own_normed = (own_hat * gain).astype(bf16)
    own_mix = columns_of(up_weight, head * head_dim)
    own_gate = columns_of(up_weight, inner + head * head_dim)
    own_bg = out_grad.astype(bf16)
    unit = down_weight.shape[0] // ctx
    units = [
        ((h * dp + d) * copies + r, d * ctx + h * copies + r)
        for h in range(heads)
        for d in range(dp)
        for r in range(copies)
    ]
    w_mix = lax.all_gather(own_mix, "dp", axis=0, tiled=True)
    hops = [pass_on((own_normed, own_normed), "ctx", 1)]
    hops[0], own_normed, own_gate = fence(hops[0], own_normed, own_gate)
    w_gate = lax.all_gather(own_gate, "dp", axis=0, tiled=True)
    for s in range(2, ctx):
        hops.append(pass_on(hops[-1], "ctx", s))
        if s < ctx - 1:
            hops[-1], w_mix, down_weight = fence(hops[-1], w_mix, down_weight)
    w_down = lax.all_gather(down_weight, "dp", axis=0, tiled=True)
    hops, w_mix, own_bg = fence(hops, w_mix, own_bg)

    conv_taps = columns_of(conv_weight, head * head_dim).astype(f32)
    conv_shift = columns_of(conv_bias, head * head_dim).astype(f32)[None]
    skip = columns_of(skip_weight, head * head_dim).astype(f32)[None]
    out_gain = columns_of(outnorm_weight, head * head_dim).astype(f32)[None]
    maps = lax.dynamic_slice_in_dim(qkv_weight, head, 1, axis=1).astype(f32)
    maps = maps.reshape(3 * block * block, head_dim // block)
    gate_rows = columns_of(gate_weight.reshape(2 * heads, 3, inner), head * head_dim)
    gate_rows = gate_rows.transpose(1, 0, 2)
    turned = gate_rows.reshape(3, 2, heads, head_dim).transpose(0, 2, 1, 3)
    turned = jnp.concatenate([turned, turned], axis=1)
    turned = lax.dynamic_slice_in_dim(turned, head, heads, axis=1)
    turned = turned.reshape(3, 2 * heads, head_dim)
    key_scale = head_dim ** (-0.5)
    pack_rows = -(-(taps + 4 + 3 * block + 6 * heads) // dp) * dp

    bg_hops = [pass_on((own_bg, own_bg), "ctx", 1)]
    normed = in_turn(own_normed, hops, "ctx")
    mixer = dot_nn(normed, w_mix).astype(bf16)
    pre, queries, keys, values, gate_part = front(
        place, mixer, conv_taps, conv_shift, maps, gate_rows, key_scale, span
    )
    bg_hops, normed, mixer, pre, gate_part = fence(bg_hops, normed, mixer, pre, gate_part)
    gate_parts = spread(gate_part, "ctx", range(ctx))
    gate_in = dot_nn(normed, w_gate)
    gate = gates(head, gate_parts, gate_bias.astype(f32)[:, None], span, share)
    bg_hops, gate, gate_in = fence(bg_hops, gate, gate_in)
    for s in range(2, ctx - 1):
        bg_hops.append(pass_on(bg_hops[-1], "ctx", s))
    mix, num, hidden = cell(
        place, gate, queries, keys, values, pre, gate_in, skip, out_gain, span
    )
    bg_hops, mix, num, hidden = fence(bg_hops, mix, num, hidden)
    bg_hops.append(pass_on(bg_hops[-1], "ctx", ctx - 1))
    w_down = lax.dynamic_slice_in_dim(w_down, head * head_dim, head_dim, axis=0)
    branch = (dot_nn(hidden, w_down) * share).astype(bf16)
    bg_hops, branch, hidden, w_down = fence(bg_hops, branch, hidden, w_down)
    branch_blocks = by_offset(branch)
    moving = scatter_on(branch_blocks, None, "ctx", 1)
    bg = in_turn(own_bg, bg_hops, "ctx")
    down_grad = dot_tn(hidden, bg).astype(bf16)
    down_grad, bg = fence(down_grad, bg)
    down_part = lax.psum_scatter(down_grad, "dp", scatter_dimension=0, tiled=True)
    num_grad, gate_in_grad, conv_tail, tail_sums = tail_back(
        place, bg, num, pre, gate_in, w_down, skip, out_gain, span
    )
    num_grad, gate_in_grad, moving = fence(num_grad, gate_in_grad, moving)
    moving = scatter_on(branch_blocks, moving, "ctx", 2)
    up_gate = dot_tn(normed, gate_in_grad).astype(bf16)
    num_grad, up_gate, gate_in_grad = fence(num_grad, up_gate, gate_in_grad)
    gate_grad_part = lax.psum_scatter(up_gate, "dp", scatter_dimension=0, tiled=True)
    dq, dk, dv, gate_own = cell_back(gate, queries, keys, values, mix, num_grad, span)
    dq, gate_own, moving, gate_in_grad, down_part = fence(
        dq, gate_own, moving, gate_in_grad, down_part
    )
    gate_grads = spread(gate_own, "ctx", range(0, ctx, copies))
    gate_normed = dot_nt(gate_in_grad, w_gate)
    gain_part = jnp.sum(up_gate.astype(f32) * w_gate.astype(f32), axis=1)
    dq, gate_grads, moving, gate_normed, gain_part = fence(
        dq, gate_grads, moving, gate_normed, gain_part
    )
    for s in range(3, ctx):
        moving = scatter_on(branch_blocks, moving, "ctx", s)
    down_part = lax.dynamic_slice_in_dim(down_part, (ctx_index % copies) * unit, unit, axis=0)
    down_part = lax.ppermute(down_part, ("dp", "ctx"), [(b, a) for a, b in units])
    mixer_grad, pack = back(
        place, dq, dk, dv, gate_grads, queries, keys, values, pre, mixer, conv_tail,
        conv_taps, maps, turned, tail_sums, key_scale, span, pack_rows,
    )
    mixer_grad, moving, pack, down_part = fence(mixer_grad, moving, pack, down_part)
    down_hops = [pass_on((down_part, down_part), "ctx", 1)]
    up_mix = mix_grads(normed, mixer_grad, w_mix, gain_part, pack, dp)
    up_mix, mixer_grad, gate_grad_part = fence(up_mix, mixer_grad, gate_grad_part)
    mix_grad_part = lax.psum_scatter(up_mix, "dp", scatter_dimension=0, tiled=False)
    gate_hops = [pass_on((gate_grad_part, gate_grad_part), "ctx", 1)]
    normed_part = ((dot_nt(mixer_grad, w_mix) + gate_normed) * share).astype(bf16)
    normed_part, down_hops, gate_hops, moving = fence(normed_part, down_hops, gate_hops, moving)
    normed_blocks = by_offset(normed_part)
    outputs = (live * (x_own + scatter_sum(branch_blocks[0], moving))).astype(bf16)[None]
    moving = None
    mix_hops = []
    for s in range(1, ctx):
        moving = scatter_on(normed_blocks, moving, "ctx", s)
        for hops in (down_hops, gate_hops):
            if len(hops) < ctx - 1:
                hops.append(pass_on(hops[-1], "ctx", len(hops) + 1))
        if s > 1:
            have = mix_hops[-1] if mix_hops else (mix_grad_part, mix_grad_part)
            mix_hops.append(pass_on(have, "ctx", s - 1))
        if s == 1:
            moving, down_hops, gate_hops, outputs, mix_grad_part = fence(
                moving, down_hops, gate_hops, outputs, mix_grad_part
            )
            small = mix_grad_part[width // dp :][: pack_rows // dp + 1].astype(f32)
            mix_grad_part = mix_grad_part[: width // dp]
        elif s == 2:
            small = lax.all_gather(after(small, *gate_hops[-1]), "dp", axis=0)
            moving, down_hops, gate_hops, mix_hops, small = fence(
                moving, down_hops, gate_hops, mix_hops, small
            )
        else:
            if s == 3:
                small = lax.all_gather(after(small, *mix_hops[-1]), "ctx", axis=0)
            moving, down_hops, gate_hops, mix_hops, small = fence(
                moving, down_hops, gate_hops, mix_hops, small
            )
    mix_hops.append(pass_on(mix_hops[-1], "ctx", ctx - 1))
    normed_grad = scatter_sum(normed_blocks[0], moving)
    input_grad = (out_grad + normalize_back(normed_grad * gain, own_hat, own_scale))[None]
    down_total = assemble_rows(place, down_part, down_hops)
    totals = unpack(small, gain, taps, heads, block)
    bias_total = totals[5][0, : 2 * heads].reshape(heads, 2).T.reshape(-1)
    up_total = assemble(place, mix_grad_part, mix_hops, gate_grad_part, gate_hops, copies)
    return (
        outputs,
        input_grad,
        totals[0].reshape(-1),
        up_total,
        totals[1],
        totals[2].reshape(-1),
        totals[3],
        totals[4],
        bias_total,
        totals[6].reshape(-1),
        totals[7].reshape(-1),
        down_total,
    )


def solution(mesh):
    rows = P("dp", "ctx", None)
    weights = P("dp", None)
    return jax.shard_map(
        on_device,
        mesh=mesh,
        in_specs=(rows, P("dp"), P(), weights, *[P()] * 7, weights, rows),
        out_specs=(rows, rows, P(), weights, *[P()] * 7, weights),
        check_vma=False,
    )
```

```python
from functools import partial

import jax
import jax.numpy as jnp
from jax import lax
from jax.experimental import pallas as pl
from jax.experimental.pallas import tpu as pltpu
from jax.sharding import PartitionSpec as P

epsilon = 1e-05
f32 = jnp.float32
bf16 = jnp.bfloat16


def dot_nn(a, b):
    return lax.dot_general(a, b, (((1,), (0,)), ((), ())), preferred_element_type=f32)


def dot_nt(a, b):
    return lax.dot_general(a, b, (((1,), (1,)), ((), ())), preferred_element_type=f32)


def dot_tn(a, b):
    return lax.dot_general(a, b, (((0,), (0,)), ((), ())), preferred_element_type=f32)


def normalize(rows):
    centred = rows - jnp.mean(rows, axis=-1, keepdims=True)
    scale = lax.rsqrt(jnp.mean(centred * centred, axis=-1, keepdims=True) + epsilon)
    return centred * scale, scale


def normalize_back(grad, normed, scale):
    return scale * (
        grad
        - jnp.mean(grad, axis=-1, keepdims=True)
        - normed * jnp.mean(grad * normed, axis=-1, keepdims=True)
    )


def silu_parts(x):
    sig = jax.nn.sigmoid(x)
    return sig, x * sig


def fold8(x):
    rows = x.shape[0]
    out = x[0:8]
    for at in range(8, rows, 8):
        out = out + x[at : at + 8]
    return out


def whole(shape):
    return pl.BlockSpec(shape, lambda *g: (0,) * len(shape), pipeline_mode=pl.Buffered(1))


def call(kernel, place, grid, in_specs, out_specs, out_shape, scratch, estimate, name, *args):
    return pl.pallas_call(
        kernel,
        grid_spec=pltpu.PrefetchScalarGridSpec(
            num_scalar_prefetch=1,
            grid=(grid,),
            in_specs=in_specs,
            out_specs=out_specs,
            scratch_shapes=scratch,
        ),
        out_shape=out_shape,
        compiler_params=kernel_params(),
        cost_estimate=estimate,
        name=name,
    )(place, *args)


def kernel_params(limit=48):
    return pltpu.CompilerParams(
        dimension_semantics=("arbitrary",), vmem_limit_bytes=limit * 1024 * 1024
    )


def cost(flops, moved, transcendentals=0):
    return pl.CostEstimate(
        flops=int(flops), bytes_accessed=int(moved), transcendentals=int(transcendentals)
    )


def row_chunks(rows, size, body, together=1):
    def step(n, carry):
        for m in range(together):
            body(pl.multiple_of((n * together + m) * size, size))
        return carry

    lax.fori_loop(0, rows // (size * together), step, 0)


def front_kernel(
    key_scale, at_ref, mix_ref, prev_ref, taps_ref, shift_ref, maps_ref, gates_ref,
    pre_ref, q_ref, k_ref, v_ref, part_ref, pad_ref,
):
    rows, width = mix_ref.shape
    taps = taps_ref.shape[0]
    lanes = maps_ref.shape[1]
    block = width // lanes
    first = pl.program_id(0) == 0
    before = prev_ref[...].astype(f32)[prev_ref.shape[0] - 8 :]
    pad_ref[0:8, :] = jnp.where(first, jnp.zeros_like(before), before)
    pad_ref[8 : 8 + rows, :] = mix_ref[...].astype(f32)

    def chunk(at):
        size = 32
        conv, mixed = [], []
        for i in range(block):
            cols = slice(i * lanes, (i + 1) * lanes)
            x = pad_ref[pl.ds(at, size + 8), cols]
            pre = shift_ref[:, cols]
            for j in range(taps):
                lag = taps - 1 - j
                pre = pre + taps_ref[j : j + 1, cols] * x[8 - lag : 8 - lag + size]
            pre_ref[pl.ds(at, size), cols] = pre
            conv.append(silu_parts(pre)[1])
            mixed.append(x[8:])

        def mapped(m, parts, o):
            out = parts[0] * maps_ref[m * block * block + o : m * block * block + o + 1, :]
            for i in range(1, block):
                r = (m * block + i) * block + o
                out = out + parts[i] * maps_ref[r : r + 1, :]
            return out

        for o in range(block):
            cols = slice(o * lanes, (o + 1) * lanes)
            q_ref[pl.ds(at, size), cols] = mapped(0, conv, o).astype(bf16)
            k_ref[pl.ds(at, size), cols] = (mapped(1, conv, o) * key_scale).astype(bf16)
            v_ref[pl.ds(at, size), cols] = mapped(2, mixed, o).astype(bf16)

    row_chunks(rows, 32, chunk)
    part_ref[...] = (
        dot_nt(gates_ref[0], q_ref[...])
        + dot_nt(gates_ref[1], k_ref[...])
        + dot_nt(gates_ref[2], v_ref[...])
    )


def front(place, mixer, conv_taps, conv_shift, maps, gate_rows, key_scale, span):
    total, width = mixer.shape
    count = total // span
    step = span // 16

    def own(i, at):
        return (lax.rem(i + count - at[0], count), 0)

    def ahead(i, at):
        return (lax.rem(i + count - 1 - at[0] + count, count) * step + step - 1, 0)

    tile = pl.BlockSpec((span, width), lambda i, at: (i, 0))
    gates_of = gate_rows.shape[1]
    return call(
        partial(front_kernel, key_scale),
        place,
        count,
        [
            pl.BlockSpec((span, width), own),
            pl.BlockSpec((16, width), ahead),
            whole(conv_taps.shape),
            whole(conv_shift.shape),
            whole(maps.shape),
            whole(gate_rows.shape),
        ],
        [tile, tile, tile, tile, pl.BlockSpec((gates_of, span), lambda i, at: (0, i))],
        [
            jax.ShapeDtypeStruct((total, width), f32),
            *[jax.ShapeDtypeStruct((total, width), bf16)] * 3,
            jax.ShapeDtypeStruct((gates_of, total), f32),
        ],
        [pltpu.VMEM((span + 8, width), f32)],
        cost(6e9, 12 * total * width, total * width),
        "front",
        mixer, mixer, conv_taps, conv_shift, maps, gate_rows,
    )


def gates_kernel(span, share, head_ref, *refs):
    parts, bias_ref, out_ref = refs[:-2], refs[-2], refs[-1]
    pre = parts[0][...]
    for p in parts[1:]:
        pre = pre + p[...]
    if share != 1.0:
        pre = pre * share
    pre = pre + bias_ref[...]
    rows, total = pre.shape
    head = head_ref[0]
    at = lax.broadcasted_iota(jnp.int32, pre.shape, 0)
    lane = lax.broadcasted_iota(jnp.int32, (8, total), 1)
    in_gate = jnp.sum(jnp.where(at == head, pre, 0.0), axis=0, keepdims=True)
    forget = jnp.sum(jnp.where(at == head + rows // 2, pre, 0.0), axis=0, keepdims=True)
    forget = jnp.broadcast_to(forget, (8, total))
    log_forget = jnp.minimum(forget, 0.0) - jnp.log1p(jnp.exp(-jnp.abs(forget)))
    place = lane % span
    running = log_forget
    by = 1
    while by < span:
        running = running + jnp.where(place >= by, pltpu.roll(running, by, 1), 0.0)
        by *= 2
    whole_sum = jnp.where(place == span - 1, running, 0.0)
    by = 1
    while by < span:
        whole_sum = whole_sum + pltpu.roll(whole_sum, total - by, 1) * jnp.where(
            place < span - by, 1.0, 0.0
        )
        by *= 2
    out_ref[0:1, :] = in_gate
    out_ref[1:2, :] = running[0:1]
    out_ref[2:3, :] = whole_sum[0:1]
    out_ref[3:4, :] = jax.nn.sigmoid(-forget)[0:1]
    out_ref[4:8, :] = jnp.zeros((4, total), f32)


def gates(head, parts, bias, span, share):
    rows, total = parts[0].shape
    full = pl.BlockSpec((rows, total), lambda i, s: (0, 0))
    return pl.pallas_call(
        partial(gates_kernel, span, share),
        grid_spec=pltpu.PrefetchScalarGridSpec(
            num_scalar_prefetch=1,
            grid=(1,),
            in_specs=[full] * len(parts) + [pl.BlockSpec((rows, 1), lambda i, s: (0, 0))],
            out_specs=pl.BlockSpec((8, total), lambda i, s: (0, 0)),
        ),
        out_shape=jax.ShapeDtypeStruct((8, total), f32),
        name="gates",
    )(head.reshape(1).astype(jnp.int32), *parts, bias)


def column_of(row):
    n = row.shape[1]
    eye = lax.broadcasted_iota(jnp.int32, (n, n), 0) == lax.broadcasted_iota(jnp.int32, (n, n), 1)
    return jnp.sum(jnp.where(eye, jnp.broadcast_to(row, (n, n)), 0.0), axis=1, keepdims=True)


def row_of(column):
    n = column.shape[0]
    eye = lax.broadcasted_iota(jnp.int32, (n, n), 0) == lax.broadcasted_iota(jnp.int32, (n, n), 1)
    return jnp.sum(jnp.where(eye, jnp.broadcast_to(column, (n, n)), 0.0), axis=0, keepdims=True)


def tile_weights(gate_ref, column, reach, lanes, n, causal):
    row = gate_ref[0:1, lanes] - gate_ref[1:2, lanes] + reach
    exponent = column + row
    if not causal:
        return jnp.exp(exponent)
    keep = lax.broadcasted_iota(jnp.int32, (n, n), 0) >= lax.broadcasted_iota(jnp.int32, (n, n), 1)
    return jnp.where(keep, jnp.exp(jnp.where(keep, exponent, 0.0)), 0.0)


def cell_kernel(
    at_ref, gate_ref, q_ref, k_ref, v_ref, pre_ref, gin_ref, skip_ref, og_ref,
    mix_ref, num_ref, hid_ref,
):
    n, width = q_ref.shape
    tb = pl.program_id(0)
    here = pl.ds(pl.multiple_of(tb * n, n), n)
    column = column_of(gate_ref[1:2, here])

    def one(sb, reach, causal):
        lanes = pl.ds(pl.multiple_of(sb * n, n), n)
        w = tile_weights(gate_ref, column, reach, lanes, n, causal)
        mix = (w * dot_nt(q_ref[...], k_ref[lanes, :])).astype(bf16)
        mix_ref[:, lanes] = mix
        return dot_nn(mix, v_ref[lanes, :])

    num_ref[...] = one(tb, jnp.zeros((1, n), f32), True)

    def earlier(step, reach):
        sb = tb - 1 - step
        reach = reach + gate_ref[2:3, pl.ds(pl.multiple_of(sb * n, n), n)]
        num_ref[...] += one(sb, reach, False)
        return reach

    lax.fori_loop(0, tb, earlier, jnp.zeros((1, n), f32))
    skip, og = skip_ref[...], og_ref[...]

    def chunk(at):
        rows = pl.ds(at, 16)
        hat, _ = normalize(num_ref[rows, :])
        conv = silu_parts(pre_ref[rows, :])[1]
        act = silu_parts(gin_ref[rows, :])[1]
        hid_ref[rows, :] = ((hat * og + skip * conv) * act).astype(bf16)

    row_chunks(n, 16, chunk, 8)


def cell(place, gate, q, k, v, pre, gate_in, skip, out_gain, span):
    total, width = q.shape
    count = total // span

    def own(i, at):
        return (lax.rem(i + count - at[0], count), 0)

    tile = pl.BlockSpec((span, width), lambda i, at: (i, 0))
    moved = pl.BlockSpec((span, width), own)
    full = whole((total, width))
    return call(
        cell_kernel,
        place,
        count,
        [whole(gate.shape), tile, full, full, tile, moved, whole(skip.shape), whole(out_gain.shape)],
        [pl.BlockSpec((span, total), lambda i, at: (i, 0)), tile, moved],
        [
            jax.ShapeDtypeStruct((total, total), bf16),
            jax.ShapeDtypeStruct((total, width), f32),
            jax.ShapeDtypeStruct((total, width), bf16),
        ],
        [],
        cost(2.5 * total * width * total, 20 * total * width, 3 * total * width),
        "cell",
        gate, q, k, v, pre, gate_in, skip, out_gain,
    )


def tail_back_kernel(
    at_ref, bg_ref, num_ref, pre_ref, gin_ref, down_ref, skip_ref, og_ref,
    ng_ref, gg_ref, ct_ref, sums_ref, hg_ref,
):
    hg_ref[...] = dot_nt(bg_ref[...], down_ref[...])

    @pl.when(pl.program_id(0) == 0)
    def _():
        sums_ref[...] = jnp.zeros_like(sums_ref)

    skip, og = skip_ref[...], og_ref[...]

    def chunk(at):
        rows = pl.ds(at, 16)
        hat, scale = normalize(num_ref[rows, :])
        conv = silu_parts(pre_ref[rows, :])[1]
        before = hat * og + skip * conv
        gin = gin_ref[rows, :]
        sig, act = silu_parts(gin)
        hg = hg_ref[rows, :]
        gg_ref[rows, :] = (hg * before * (sig * (1.0 + gin * (1.0 - sig)))).astype(bf16)
        bgrad = hg * act
        sums_ref[0:8, :] += fold8(bgrad * conv)
        sums_ref[8:16, :] += fold8(bgrad * hat)
        ct_ref[rows, :] = bgrad * skip
        ng_ref[rows, :] = normalize_back(bgrad * og, hat, scale).astype(bf16)

    row_chunks(hg_ref.shape[0], 16, chunk, 8)


def tail_back(place, bg, num, pre, gate_in, w_down, skip, out_gain, span):
    model = bg.shape[1]
    total, width = num.shape
    count = total // span

    def own(i, at):
        return (lax.rem(i + count - at[0], count), 0)

    tile = pl.BlockSpec((span, width), lambda i, at: (i, 0))
    moved = pl.BlockSpec((span, width), own)
    return call(
        tail_back_kernel,
        place,
        count,
        [
            pl.BlockSpec((span, model), own), tile, tile, moved,
            whole(w_down.shape), whole(skip.shape), whole(out_gain.shape),
        ],
        [tile, moved, tile, pl.BlockSpec((16, width), lambda i, at: (0, 0))],
        [
            jax.ShapeDtypeStruct((total, width), bf16),
            jax.ShapeDtypeStruct((total, width), bf16),
            jax.ShapeDtypeStruct((total, width), f32),
            jax.ShapeDtypeStruct((16, width), f32),
        ],
        [pltpu.VMEM((span, width), f32)],
        cost(2 * total * model * width, 24 * total * width, 2 * total * width),
        "tail_back",
        bg, num, pre, gate_in, w_down, skip, out_gain,
    )


def cell_back_kernel(
    gate_ref, q_ref, k_ref, v_ref, mix_ref, ng_ref,
    dq_ref, dk_ref, dv_ref, gout_ref, sums_ref,
):
    n, width = q_ref.shape
    total = k_ref.shape[0]
    tb = pl.program_id(0)
    here = pl.ds(pl.multiple_of(tb * n, n), n)
    column = column_of(gate_ref[1:2, here])

    @pl.when(tb == 0)
    def _():
        sums_ref[...] = jnp.zeros_like(sums_ref)

    def one(sb, reach, causal):
        lanes = pl.ds(pl.multiple_of(sb * n, n), n)
        w = tile_weights(gate_ref, column, reach, lanes, n, causal)
        mix = mix_ref[:, lanes]
        ng = ng_ref[...]
        mix_grad = dot_nt(ng, v_ref[lanes, :])
        exponent_grad = mix_grad * mix.astype(f32)
        scores_grad = (w * mix_grad).astype(bf16)
        sums_ref[0:1, lanes] += jnp.sum(exponent_grad, axis=0, keepdims=True)
        return (
            jnp.sum(exponent_grad, axis=1, keepdims=True),
            dot_nn(scores_grad, k_ref[lanes, :]),
            dot_tn(scores_grad, q_ref[...]),
            dot_tn(mix, ng),
            lanes,
        )

    by_row, dq, dk, dv, lanes = one(tb, jnp.zeros((1, n), f32), True)
    dq_ref[...] = dq
    dk_ref[lanes, :] = dk
    dv_ref[lanes, :] = dv

    def earlier(step, carry):
        reach, by_row = carry
        sb = tb - 1 - step
        reach = reach + gate_ref[2:3, pl.ds(pl.multiple_of(sb * n, n), n)]
        more, dq, dk, dv, lanes = one(sb, reach, False)
        dq_ref[...] += dq
        dk_ref[lanes, :] += dk
        dv_ref[lanes, :] += dv
        return reach, by_row + more

    _, by_row = lax.fori_loop(0, tb, earlier, (jnp.zeros((1, n), f32), by_row))
    sums_ref[1:2, here] = row_of(by_row)

    @pl.when(tb == pl.num_programs(0) - 1)
    def _():
        by_source = sums_ref[0:1, :]
        lane = lax.broadcasted_iota(jnp.int32, (8, total), 1)
        running = jnp.broadcast_to(sums_ref[1:2, :] - by_source, (8, total))
        by = 1
        while by < total:
            running = running + jnp.where(
                lane < total - by, pltpu.roll(running, total - by, 1), 0.0
            )
            by *= 2
        gout_ref[0:1, :] = by_source
        gout_ref[1:2, :] = running[0:1] * gate_ref[3:4, :]


def cell_back(gate, q, k, v, mix, num_grad, span):
    total, width = q.shape
    tile = pl.BlockSpec((span, width), lambda i: (i, 0))
    full = whole((total, width))
    return pl.pallas_call(
        cell_back_kernel,
        grid=(total // span,),
        in_specs=[
            whole(gate.shape), tile, full, full,
            pl.BlockSpec((span, total), lambda i: (i, 0)), tile,
        ],
        out_specs=[
            tile,
            pl.BlockSpec((total, width), lambda i: (0, 0)),
            pl.BlockSpec((total, width), lambda i: (0, 0)),
            pl.BlockSpec((2, total), lambda i: (0, 0)),
        ],
        out_shape=[
            *[jax.ShapeDtypeStruct((total, width), f32)] * 3,
            jax.ShapeDtypeStruct((2, total), f32),
        ],
        scratch_shapes=[pltpu.VMEM((8, total), f32)],
        compiler_params=kernel_params(),
        cost_estimate=cost(
            5 * total * total * width, 24 * total * width, total * total
        ),
        name="cell_back",
    )(gate, q, k, v, mix, num_grad)


def back_kernel(
    key_scale, heads, at_ref, dq_ref, dk_ref, dv_ref, q_ref, k_ref, v_ref, pre_ref, mix_ref, ct_ref,
    taps_ref, maps_ref, gates_ref, *refs,
):
    gate_parts, sums_ref = refs[:heads], refs[heads]
    mg_ref, pack_ref, tg_ref, wg_ref, grow_ref, gsum_ref, gb_ref, pg_ref, mv_ref = refs[heads + 1 :]
    rows, width = dq_ref.shape
    taps = taps_ref.shape[0]
    lanes = maps_ref.shape[1]
    block = width // lanes
    per_map = block * block

    @pl.when(pl.program_id(0) == 0)
    def _():
        tg_ref[...] = jnp.zeros_like(tg_ref)
        wg_ref[...] = jnp.zeros_like(wg_ref)
        grow_ref[...] = jnp.zeros_like(grow_ref)
        gsum_ref[...] = jnp.zeros_like(gsum_ref)
        pg_ref[rows : rows + 8, :] = jnp.zeros((8, width), f32)

    gg = jnp.concatenate([p[...] for p in gate_parts], axis=0)
    gsum_ref[...] += jnp.broadcast_to(jnp.sum(gg, axis=1, keepdims=True), gsum_ref.shape)
    high = gg.astype(bf16)
    low = (gg - high.astype(f32)).astype(bf16)
    both = jnp.concatenate([high, low], axis=0)
    for m, x_ref in enumerate((q_ref, k_ref, v_ref)):
        gb_ref[m] = dot_tn(both, gates_ref[m])
        grow = dot_nn(both, x_ref[...])
        grow_ref[m] += grow[: 2 * heads] + grow[2 * heads :]

    size = 32

    def chunk(at):
        here = pl.ds(at, size)

        def cols(i):
            return slice(i * lanes, (i + 1) * lanes)

        def weight(m, i, o):
            r = (m * block + i) * block + o
            return maps_ref[r : r + 1, :]

        pre = [pre_ref[here, cols(i)] for i in range(block)]
        parts = [silu_parts(p) for p in pre]
        conv_grad = [ct_ref[here, cols(i)] for i in range(block)]
        for m, (g_ref, scale) in enumerate(((dq_ref, None), (dk_ref, key_scale))):
            for o in range(block):
                g = g_ref[here, cols(o)] + gb_ref[m, here, cols(o)]
                if scale is not None:
                    g = g * scale
                for i in range(block):
                    conv_grad[i] = conv_grad[i] + g * weight(m, i, o)
                    wg_ref[m * per_map + i * block + o] += fold8(parts[i][1] * g)
        for i in range(block):
            sig = parts[i][0]
            pg_ref[here, cols(i)] = conv_grad[i] * (sig * (1.0 + pre[i] * (1.0 - sig)))
        mixed = [mix_ref[here, cols(i)].astype(f32) for i in range(block)]
        grads = [None] * block
        for o in range(block):
            g = dv_ref[here, cols(o)] + gb_ref[2, here, cols(o)]
            for i in range(block):
                term = g * weight(2, i, o)
                grads[i] = term if grads[i] is None else grads[i] + term
                wg_ref[2 * per_map + i * block + o] += fold8(mixed[i] * g)
        for i in range(block):
            mv_ref[here, cols(i)] = grads[i]

    row_chunks(rows, size, chunk)

    def second(at):
        here = pl.ds(at, size)
        for i in range(block):
            cols = slice(i * lanes, (i + 1) * lanes)
            x = pg_ref[pl.ds(at, size + 8), cols]
            m = mix_ref[here, cols].astype(f32)
            grad = mv_ref[here, cols]
            for j in range(taps):
                lead = taps - 1 - j
                moved = x[lead : lead + size]
                grad = grad + taps_ref[j : j + 1, cols] * moved
                tg_ref[j, :, cols] += fold8(moved * m)
            tg_ref[taps, :, cols] += fold8(x[0:size])
            mg_ref[here, cols] = grad.astype(bf16)

    row_chunks(rows, size, second)
    pg_ref[rows : rows + 8, :] = pg_ref[0:8, :]

    @pl.when(pl.program_id(0) == pl.num_programs(0) - 1)
    def _():
        pack_ref[...] = jnp.zeros_like(pack_ref)
        at = 0
        for j in range(taps + 1):
            pack_ref[at : at + 1, :] = jnp.sum(tg_ref[j], axis=0, keepdims=True)
            at += 1
        for r in range(3 * block):
            for o in range(block):
                pack_ref[at : at + 1, o * lanes : (o + 1) * lanes] = jnp.sum(
                    wg_ref[r * block + o], axis=0, keepdims=True
                )
            at += 1
        for m in range(3):
            pack_ref[at : at + 2 * heads, :] = grow_ref[m]
            at += 2 * heads
        for j in range(2):
            pack_ref[at : at + 1, :] = jnp.sum(sums_ref[8 * j : 8 * j + 8], axis=0, keepdims=True)
            at += 1
        sums = gsum_ref[...]
        diagonal = lax.broadcasted_iota(jnp.int32, sums.shape, 0) == lax.broadcasted_iota(
            jnp.int32, sums.shape, 1
        )
        pack_ref[at : at + 1, 0:128] = jnp.sum(
            jnp.where(diagonal, sums, 0.0), axis=0, keepdims=True
        )


def back(
    place, dq, dk, dv, gate_parts, q, k, v, pre, mixer, conv_tail, conv_taps, maps, gate_rows,
    tail_sums, key_scale, span, pack_rows,
):
    total, width = dq.shape
    count = total // span
    taps = conv_taps.shape[0]
    lanes = maps.shape[1]
    heads = len(gate_parts)

    def own(i, at):
        return (lax.rem(2 * count - 1 - i - at[0], count), 0)

    tile = pl.BlockSpec((span, width), lambda i, at: (count - 1 - i, 0))
    moved = pl.BlockSpec((span, width), own)
    return call(
        partial(back_kernel, key_scale, heads),
        place,
        count,
        [
            tile, tile, tile, tile, tile, tile, tile, moved, tile,
            whole(conv_taps.shape), whole(maps.shape), whole(gate_rows.shape),
            *[pl.BlockSpec((2, span), lambda i, at: (0, count - 1 - i))] * heads,
            whole(tail_sums.shape),
        ],
        [moved, pl.BlockSpec((pack_rows, width), lambda i, at: (0, 0))],
        [
            jax.ShapeDtypeStruct((total, width), bf16),
            jax.ShapeDtypeStruct((pack_rows, width), f32),
        ],
        [
            pltpu.VMEM((taps + 1, 8, width), f32),
            pltpu.VMEM((maps.shape[0], 8, lanes), f32),
            pltpu.VMEM((3, 2 * heads, width), f32),
            pltpu.VMEM((2 * heads, 128), f32),
            pltpu.VMEM((3, span, width), f32),
            pltpu.VMEM((span + 8, width), f32),
            pltpu.VMEM((span, width), f32),
        ],
        cost(12e9, 30 * total * width, 2 * total * width),
        "back",
        dq, dk, dv, q, k, v, pre, mixer, conv_tail, conv_taps, maps, gate_rows, *gate_parts,
        tail_sums,
    )


def assemble_kernel(count, at_ref, *refs):
    out_ref = refs[-1]
    inputs = refs[:-1]
    step = pl.program_id(0)
    halves = len(inputs) // (2 * count - 1)
    for half in range(halves):
        own, others = inputs[half * (2 * count - 1)], inputs[half * (2 * count - 1) + 1 : (half + 1) * (2 * count - 1)]
        at = half * count

        @pl.when(step == at)
        def _(ref=own):
            out_ref[...] = ref[...].astype(out_ref.dtype)

        for r in range(1, count):
            ahead, behind = others[2 * (r - 1)], others[2 * (count - r - 1) + 1]

            @pl.when((step == at + r) & (at_ref[0] + r < count))
            def _(ref=ahead):
                out_ref[...] = ref[...].astype(out_ref.dtype)

            @pl.when((step == at + r) & (at_ref[0] + r >= count))
            def _(ref=behind):
                out_ref[...] = ref[...].astype(out_ref.dtype)


def flat(own, hops):
    return [own] + [x for pair in hops for x in pair]


def assemble(place, own_mix, mix_hops, own_gate, gate_hops, copies):
    rows, width = own_mix.shape
    count = len(mix_hops) + 1
    heads = count // copies

    def out_map(i, at):
        half = i // count
        source = lax.rem(i - half * count + at[0], count)
        return (0, half * heads + source // copies)

    parts = flat(own_mix, mix_hops) + flat(own_gate, gate_hops)
    return call(
        partial(assemble_kernel, count),
        place,
        2 * count,
        [whole((rows, width))] * len(parts),
        pl.BlockSpec((rows, width), out_map),
        jax.ShapeDtypeStruct((rows, 2 * heads * width), f32),
        [],
        cost(0, 12 * count * rows * width),
        "assemble",
        *parts,
    )


def assemble_rows(place, own, hops):
    rows, width = own.shape
    count = len(hops) + 1
    parts = flat(own, hops)
    return call(
        partial(assemble_kernel, count),
        place,
        count,
        [whole((rows, width))] * len(parts),
        pl.BlockSpec((rows, width), lambda i, at: (lax.rem(i + at[0], count), 0)),
        jax.ShapeDtypeStruct((count * rows, width), f32),
        [],
        cost(0, 6 * count * rows * width),
        "assemble_rows",
        *parts,
    )


def mix_grads_kernel(x_ref, g_ref, pack_ref, out_ref):
    rows = x_ref.shape[1]
    out_ref[0, :rows, :] = dot_tn(x_ref[...], g_ref[...]).astype(bf16)
    pack = pack_ref[0]
    fill = jnp.zeros((out_ref.shape[1] - rows - pack.shape[0], pack.shape[1]), f32)
    out_ref[0, rows:, :] = jnp.concatenate([pack, fill], axis=0).astype(bf16)


def mix_grads(normed, mixer_grad, pack, dp):
    total, width = normed.shape
    cols = mixer_grad.shape[1]
    rows = width // dp
    pack = pack.reshape(dp, pack.shape[0] // dp, cols)
    extra = -(-(pack.shape[1] + 1) // 16) * 16
    return pl.pallas_call(
        mix_grads_kernel,
        grid=(dp,),
        in_specs=[
            pl.BlockSpec((total, rows), lambda i: (0, i)),
            whole(mixer_grad.shape),
            pl.BlockSpec((1,) + pack.shape[1:], lambda i: (i, 0, 0)),
        ],
        out_specs=pl.BlockSpec((1, rows + extra, cols), lambda i: (i, 0, 0)),
        out_shape=jax.ShapeDtypeStruct((dp, rows + extra, cols), bf16),
        compiler_params=kernel_params(),
        cost_estimate=cost(2 * total * width * cols, 2 * (total * width + 2 * width * cols)),
        name="mix_grads",
    )(normed, mixer_grad, pack)


def unpack_kernel(per, taps, heads, block, x_ref, gain_ref, norm_ref, convw_ref, convb_ref, maps_ref, gates_ref, bias_ref, skip_ref, og_ref):
    copies = x_ref.shape[0] // heads
    dp = x_ref.shape[1]
    width = x_ref.shape[3]
    lanes = width // block
    inner = heads * width
    rows = norm_ref.shape[1] // dp

    def row(h, r):
        return x_ref[h * copies, r // per, r % per : r % per + 1, :].astype(f32)

    for d in range(dp):
        total = x_ref[0, d, per : per + 1, 0:rows].astype(f32)
        for h in range(1, heads):
            total = total + x_ref[h * copies, d, per : per + 1, 0:rows].astype(f32)
        norm_ref[:, d * rows : (d + 1) * rows] = total / gain_ref[:, d * rows : (d + 1) * rows]
    for h in range(heads):
        cols = slice(h * width, (h + 1) * width)
        for j in range(taps):
            convw_ref[j : j + 1, cols] = row(h, j)
        convb_ref[:, cols] = row(h, taps)
        at = taps + 1
        for m in range(3):
            for i in range(block):
                values = row(h, at)
                for o in range(block):
                    maps_ref[m, h, i, o : o + 1, :] = values[:, o * lanes : (o + 1) * lanes]
                at += 1
        for m in range(3):
            for j in range(heads):
                for p in range(2):
                    g = p * heads + (h + j) % heads
                    start = m * inner + h * width
                    gates_ref[g : g + 1, start : start + width] = row(h, at)
                    at += 1
        skip_ref[:, cols] = row(h, at)
        og_ref[:, cols] = row(h, at + 1)
        if h == 0:
            bias_ref[...] = row(h, at + 2)[:, 0:128]


def unpack(small, gain, per, taps, heads, block):
    width = small.shape[3]
    inner = heads * width
    shapes = [
        gain.shape, (taps, inner), (1, inner), (3, heads, block, block, width // block),
        (2 * heads, 3 * inner), (1, 128), (1, inner), (1, inner),
    ]
    return pl.pallas_call(
        partial(unpack_kernel, per, taps, heads, block),
        grid=(1,),
        in_specs=[whole(small.shape), whole(gain.shape)],
        out_specs=[pl.BlockSpec(x, lambda i, n=len(x): (0,) * n) for x in shapes],
        out_shape=[jax.ShapeDtypeStruct(x, f32) for x in shapes],
        compiler_params=kernel_params(),
        name="unpack",
    )(small, gain)


def merge(place, own, hops):
    rows, width = own.shape
    count = len(hops) + 1
    parts = flat(own, hops)
    return call(
        partial(assemble_kernel, count),
        place,
        count,
        [whole((rows, width))] * len(parts),
        pl.BlockSpec((rows, width), lambda i, at: (i, 0)),
        jax.ShapeDtypeStruct((count * rows, width), own.dtype),
        [],
        cost(0, 4 * count * rows * width),
        "merge",
        *parts,
    )


def after(x, *others):
    if isinstance(x, list):
        return list(lax.optimization_barrier((*x, *others))[: len(x)])
    return lax.optimization_barrier((x, *others))[0]


def fence(*values):
    return lax.optimization_barrier(values)


def pass_on(pair, axis, s):
    n = lax.axis_size(axis)
    return (
        lax.ppermute(pair[0], axis, [(i, i - 1) for i in range(1, n - s + 1)]),
        lax.ppermute(pair[1], axis, [(i, i + 1) for i in range(s - 1, n - 1)]),
    )


def scatter_on(blocks, moving, axis, s):
    n = lax.axis_size(axis)
    ahead, behind = blocks[n - s], blocks[s]
    if s > 1:
        ahead = (ahead.astype(f32) + moving[0].astype(f32)).astype(bf16)
        behind = (behind.astype(f32) + moving[1].astype(f32)).astype(bf16)
    return (
        lax.ppermute(ahead, axis, [(i, i + 1) for i in range(s)]),
        lax.ppermute(behind, axis, [(i, i - 1) for i in range(n - s, n)]),
    )


def scatter_sum(own, terms):
    total = own.astype(f32)
    for term in terms:
        total = total + term.astype(f32)
    return total


def spread(x, axis, offsets):
    n = lax.axis_size(axis)
    return [
        x if r == 0 else lax.ppermute(x, axis, [(i, (i - r) % n) for i in range(n)]) for r in offsets
    ]


def on_device(
    inputs,
    lengths,
    norm_gain,
    up_weight,
    conv_weight,
    conv_bias,
    qkv_weight,
    gate_weight,
    gate_bias,
    skip_weight,
    outnorm_weight,
    down_weight,
    grad_out,
):
    span = inputs.shape[1]
    width = inputs.shape[2]
    inner = conv_weight.shape[1]
    taps = conv_weight.shape[0]
    heads = qkv_weight.shape[1]
    block = qkv_weight.shape[2]
    head_dim = inner // heads
    dp = lax.axis_size("dp")
    ctx = lax.axis_size("ctx")
    copies = ctx // heads
    total = ctx * span
    ctx_index = lax.axis_index("ctx")
    place = ctx_index.reshape(1).astype(jnp.int32)
    head = ctx_index // copies
    share = 1.0 / copies

    def columns_of(w, start):
        return lax.dynamic_slice_in_dim(w, start, head_dim, axis=w.ndim - 1)

    def by_offset(x):
        return [x[r * span : (r + 1) * span] for r in range(ctx)]

    live = (ctx_index * span + jnp.arange(span) < lengths[0]).astype(f32)[:, None]
    x_own = inputs[0].astype(f32)
    out_grad = grad_out[0].astype(f32) * live
    gain = norm_gain.astype(f32)[None]
    own_hat, own_scale = normalize(x_own)
    own_normed = (own_hat * gain).astype(bf16)
    own_mix = columns_of(up_weight, head * head_dim)
    own_gate = columns_of(up_weight, inner + head * head_dim)
    own_bg = out_grad.astype(bf16)
    unit = down_weight.shape[0] // ctx
    units = [
        ((h * dp + d) * copies + r, d * ctx + h * copies + r)
        for h in range(heads)
        for d in range(dp)
        for r in range(copies)
    ]
    w_mix = lax.all_gather(own_mix, "dp", axis=0, tiled=True)
    hops = [pass_on((own_normed, own_normed), "ctx", 1)]
    hops[0], own_normed, own_gate = fence(hops[0], own_normed, own_gate)
    w_gate = lax.all_gather(own_gate, "dp", axis=0, tiled=True)
    for s in range(2, ctx):
        hops.append(pass_on(hops[-1], "ctx", s))
        if s < ctx - 1:
            hops[-1], w_mix, down_weight = fence(hops[-1], w_mix, down_weight)
    w_down = lax.all_gather(down_weight, "dp", axis=0, tiled=True)
    hops, w_mix, own_bg = fence(hops, w_mix, own_bg)

    conv_taps = columns_of(conv_weight, head * head_dim).astype(f32)
    conv_shift = columns_of(conv_bias, head * head_dim).astype(f32)[None]
    skip = columns_of(skip_weight, head * head_dim).astype(f32)[None]
    out_gain = columns_of(outnorm_weight, head * head_dim).astype(f32)[None]
    maps = lax.dynamic_slice_in_dim(qkv_weight, head, 1, axis=1).astype(f32)
    maps = maps.reshape(3 * block * block, head_dim // block)
    gate_rows = columns_of(gate_weight.reshape(2 * heads, 3, inner), head * head_dim)
    gate_rows = gate_rows.transpose(1, 0, 2)
    turned = gate_rows.reshape(3, 2, heads, head_dim).transpose(0, 2, 1, 3)
    turned = jnp.concatenate([turned, turned], axis=1)
    turned = lax.dynamic_slice_in_dim(turned, head, heads, axis=1)
    turned = turned.reshape(3, 2 * heads, head_dim)
    turned = jnp.concatenate([turned, turned], axis=1)
    key_scale = head_dim ** (-0.5)
    pack_rows = -(-(taps + 4 + 3 * block + 6 * heads) // dp) * dp

    bg_hops = [pass_on((own_bg, own_bg), "ctx", 1)]
    normed = merge(place, own_normed, hops)
    mixer = dot_nn(normed, w_mix).astype(bf16)
    gate_in = dot_nn(normed, w_gate)
    bg_hops, normed, mixer, gate_in = fence(bg_hops, normed, mixer, gate_in)
    if ctx > 3:
        bg_hops.append(pass_on(bg_hops[-1], "ctx", 2))
    pre, queries, keys, values, gate_part = front(
        place, mixer, conv_taps, conv_shift, maps, gate_rows, key_scale, span
    )
    pre, gate_part = fence(pre, gate_part)
    gate_parts = spread(gate_part, "ctx", range(ctx))
    gate = gates(head, gate_parts, gate_bias.astype(f32)[:, None], span, share)
    bg_hops, gate = fence(bg_hops, gate)
    for s in range(len(bg_hops) + 1, ctx):
        bg_hops.append(pass_on(bg_hops[-1], "ctx", s))
    mix, num, hidden = cell(
        place, gate, queries, keys, values, pre, gate_in, skip, out_gain, span
    )
    w_down = lax.dynamic_slice_in_dim(w_down, head * head_dim, head_dim, axis=0)
    branch = (dot_nn(hidden, w_down) * share).astype(bf16)
    bg_hops, branch, hidden, w_down = fence(bg_hops, branch, hidden, w_down)
    branch_blocks = by_offset(branch)
    moving = scatter_on(branch_blocks, None, "ctx", 1)
    bg = merge(place, own_bg, bg_hops)
    down_grad = dot_tn(hidden, bg).astype(bf16)
    down_grad, bg = fence(down_grad, bg)
    down_part = lax.psum_scatter(down_grad, "dp", scatter_dimension=0, tiled=True)
    num_grad, gate_in_grad, conv_tail, tail_sums = tail_back(
        place, bg, num, pre, gate_in, w_down, skip, out_gain, span
    )
    num_grad, gate_in_grad, moving = fence(num_grad, gate_in_grad, moving)
    moving = scatter_on(branch_blocks, moving, "ctx", 2)
    up_gate = dot_tn(normed, gate_in_grad).astype(bf16)
    num_grad, up_gate, gate_in_grad = fence(num_grad, up_gate, gate_in_grad)
    gate_grad_part = lax.psum_scatter(up_gate, "dp", scatter_dimension=0, tiled=True)
    dq, dk, dv, gate_own = cell_back(gate, queries, keys, values, mix, num_grad, span)
    dq, gate_own, moving, gate_in_grad, down_part = fence(
        dq, gate_own, moving, gate_in_grad, down_part
    )
    gate_grads = spread(gate_own, "ctx", range(0, ctx, copies))
    gate_normed = dot_nt(gate_in_grad, w_gate)
    dq, gate_grads, moving, gate_normed = fence(dq, gate_grads, moving, gate_normed)
    for s in range(3, ctx):
        moving = scatter_on(branch_blocks, moving, "ctx", s)
    down_part = lax.dynamic_slice_in_dim(down_part, (ctx_index % copies) * unit, unit, axis=0)
    down_part = lax.ppermute(down_part, ("dp", "ctx"), [(b, a) for a, b in units])
    mixer_grad, pack = back(
        place, dq, dk, dv, gate_grads, queries, keys, values, pre, mixer, conv_tail,
        conv_taps, maps, turned, tail_sums, key_scale, span, pack_rows,
    )
    mixer_grad, moving, pack, down_part = fence(mixer_grad, moving, pack, down_part)
    down_hops = [pass_on((down_part, down_part), "ctx", 1)]
    up_mix = mix_grads(normed, mixer_grad, pack, dp)
    up_mix, mixer_grad, gate_grad_part = fence(up_mix, mixer_grad, gate_grad_part)
    mix_grad_part = lax.psum_scatter(up_mix, "dp", scatter_dimension=0, tiled=False)
    gate_hops = [pass_on((gate_grad_part, gate_grad_part), "ctx", 1)]
    normed_part = ((dot_nt(mixer_grad, w_mix) + gate_normed) * share).astype(bf16)
    normed_part, down_hops, gate_hops, moving = fence(normed_part, down_hops, gate_hops, moving)
    normed_blocks = by_offset(normed_part)
    outputs = (live * (x_own + scatter_sum(branch_blocks[0], moving))).astype(bf16)[None]
    moving = None
    mix_hops = []
    for s in range(1, ctx):
        moving = scatter_on(normed_blocks, moving, "ctx", s)
        for hops in (down_hops, gate_hops):
            if len(hops) < ctx - 1:
                hops.append(pass_on(hops[-1], "ctx", len(hops) + 1))
        if s > 1:
            have = mix_hops[-1] if mix_hops else (mix_grad_part, mix_grad_part)
            mix_hops.append(pass_on(have, "ctx", s - 1))
        if s == 1:
            moving, down_hops, gate_hops, outputs, mix_grad_part = fence(
                moving, down_hops, gate_hops, outputs, mix_grad_part
            )
            rows = width // dp
            per = pack_rows // dp
            small = mix_grad_part[rows : rows + 16]
            mix_grad_part = mix_grad_part[:rows]
            gain_part = mix_grad_part.astype(f32) * own_mix.astype(f32)
            gain_part = gain_part + gate_grad_part.astype(f32) * own_gate.astype(f32)
            gain_part = jnp.pad(jnp.sum(gain_part, axis=1)[None], ((0, 0), (0, head_dim - rows)))
            at = lax.broadcasted_iota(jnp.int32, (16, 1), 0)
            small = jnp.where(at == per, gain_part.astype(bf16), small)[: -(-(per + 1) // 8) * 8]
        elif s == 2:
            small = lax.all_gather(after(small, *gate_hops[-1]), "dp", axis=0)
            small = lax.all_gather(small, "ctx", axis=0)
            moving, down_hops, gate_hops, mix_hops, small = fence(
                moving, down_hops, gate_hops, mix_hops, small
            )
        else:
            moving, down_hops, gate_hops, mix_hops = fence(moving, down_hops, gate_hops, mix_hops)
    mix_hops.append(pass_on(mix_hops[-1], "ctx", ctx - 1))
    normed_grad = scatter_sum(normed_blocks[0], moving)
    input_grad = (out_grad + normalize_back(normed_grad * gain, own_hat, own_scale))[None]
    down_total = assemble_rows(place, down_part, down_hops)
    totals = unpack(small, gain, per, taps, heads, block)
    bias_total = totals[5][0, : 2 * heads].reshape(heads, 2).T.reshape(-1)
    up_total = assemble(place, mix_grad_part, mix_hops, gate_grad_part, gate_hops, copies)
    return (
        outputs,
        input_grad,
        totals[0].reshape(-1),
        up_total,
        totals[1],
        totals[2].reshape(-1),
        totals[3],
        totals[4],
        bias_total,
        totals[6].reshape(-1),
        totals[7].reshape(-1),
        down_total,
    )


def solution(mesh):
    rows = P("dp", "ctx", None)
    weights = P("dp", None)
    return jax.shard_map(
        on_device,
        mesh=mesh,
        in_specs=(rows, P("dp"), P(), weights, *[P()] * 7, weights, rows),
        out_specs=(rows, rows, P(), weights, *[P()] * 7, weights),
        check_vma=False,
    )
```

```python
from functools import partial

import jax
import jax.numpy as jnp
from jax import lax
from jax.experimental import pallas as pl
from jax.experimental.pallas import tpu as pltpu
from jax.sharding import PartitionSpec as P

epsilon = 1e-05
f32 = jnp.float32
bf16 = jnp.bfloat16


def dot_nn(a, b):
    return lax.dot_general(a, b, (((1,), (0,)), ((), ())), preferred_element_type=f32)


def dot_nt(a, b):
    return lax.dot_general(a, b, (((1,), (1,)), ((), ())), preferred_element_type=f32)


def dot_tn(a, b):
    return lax.dot_general(a, b, (((0,), (0,)), ((), ())), preferred_element_type=f32)


def normalize(rows):
    centred = rows - jnp.mean(rows, axis=-1, keepdims=True)
    scale = lax.rsqrt(jnp.mean(centred * centred, axis=-1, keepdims=True) + epsilon)
    return centred * scale, scale


def normalize_back(grad, normed, scale):
    return scale * (
        grad
        - jnp.mean(grad, axis=-1, keepdims=True)
        - normed * jnp.mean(grad * normed, axis=-1, keepdims=True)
    )


def silu_parts(x):
    sig = jax.nn.sigmoid(x)
    return sig, x * sig


def fold8(x):
    rows = x.shape[0]
    out = x[0:8]
    for at in range(8, rows, 8):
        out = out + x[at : at + 8]
    return out


def whole(shape):
    return pl.BlockSpec(shape, lambda *g: (0,) * len(shape), pipeline_mode=pl.Buffered(1))


def call(kernel, place, grid, in_specs, out_specs, out_shape, scratch, estimate, name, *args):
    return pl.pallas_call(
        kernel,
        grid_spec=pltpu.PrefetchScalarGridSpec(
            num_scalar_prefetch=1,
            grid=(grid,),
            in_specs=in_specs,
            out_specs=out_specs,
            scratch_shapes=scratch,
        ),
        out_shape=out_shape,
        compiler_params=kernel_params(),
        cost_estimate=estimate,
        name=name,
    )(place, *args)


def kernel_params(limit=48):
    return pltpu.CompilerParams(
        dimension_semantics=("arbitrary",), vmem_limit_bytes=limit * 1024 * 1024
    )


def cost(flops, moved, transcendentals=0):
    return pl.CostEstimate(
        flops=int(flops), bytes_accessed=int(moved), transcendentals=int(transcendentals)
    )


def row_chunks(rows, size, body, together=1):
    def step(n, carry):
        for m in range(together):
            body(pl.multiple_of((n * together + m) * size, size))
        return carry

    lax.fori_loop(0, rows // (size * together), step, 0)


def front_kernel(
    key_scale, at_ref, mix_ref, prev_ref, taps_ref, shift_ref, maps_ref, gates_ref,
    pre_ref, q_ref, k_ref, v_ref, part_ref, pad_ref,
):
    rows, width = mix_ref.shape
    taps = taps_ref.shape[0]
    lanes = maps_ref.shape[1]
    block = width // lanes
    first = pl.program_id(0) == 0
    before = prev_ref[...].astype(f32)[prev_ref.shape[0] - 8 :]
    pad_ref[0:8, :] = jnp.where(first, jnp.zeros_like(before), before)
    pad_ref[8 : 8 + rows, :] = mix_ref[...].astype(f32)

    def chunk(at):
        size = 32
        conv, mixed = [], []
        for i in range(block):
            cols = slice(i * lanes, (i + 1) * lanes)
            x = pad_ref[pl.ds(at, size + 8), cols]
            pre = shift_ref[:, cols]
            for j in range(taps):
                lag = taps - 1 - j
                pre = pre + taps_ref[j : j + 1, cols] * x[8 - lag : 8 - lag + size]
            pre_ref[pl.ds(at, size), cols] = pre
            conv.append(silu_parts(pre)[1])
            mixed.append(x[8:])

        def mapped(m, parts, o):
            out = parts[0] * maps_ref[m * block * block + o : m * block * block + o + 1, :]
            for i in range(1, block):
                r = (m * block + i) * block + o
                out = out + parts[i] * maps_ref[r : r + 1, :]
            return out

        for o in range(block):
            cols = slice(o * lanes, (o + 1) * lanes)
            q_ref[pl.ds(at, size), cols] = mapped(0, conv, o).astype(bf16)
            k_ref[pl.ds(at, size), cols] = (mapped(1, conv, o) * key_scale).astype(bf16)
            v_ref[pl.ds(at, size), cols] = mapped(2, mixed, o).astype(bf16)

    row_chunks(rows, 32, chunk)
    part_ref[...] = (
        dot_nt(gates_ref[0], q_ref[...])
        + dot_nt(gates_ref[1], k_ref[...])
        + dot_nt(gates_ref[2], v_ref[...])
    )


def front(place, mixer, conv_taps, conv_shift, maps, gate_rows, key_scale, span):
    total, width = mixer.shape
    count = total // span
    step = span // 16

    def own(i, at):
        return (lax.rem(i + count - at[0], count), 0)

    def ahead(i, at):
        return (lax.rem(i + count - 1 - at[0] + count, count) * step + step - 1, 0)

    tile = pl.BlockSpec((span, width), lambda i, at: (i, 0))
    gates_of = gate_rows.shape[1]
    return call(
        partial(front_kernel, key_scale),
        place,
        count,
        [
            pl.BlockSpec((span, width), own),
            pl.BlockSpec((16, width), ahead),
            whole(conv_taps.shape),
            whole(conv_shift.shape),
            whole(maps.shape),
            whole(gate_rows.shape),
        ],
        [tile, tile, tile, tile, pl.BlockSpec((gates_of, span), lambda i, at: (0, i))],
        [
            jax.ShapeDtypeStruct((total, width), f32),
            *[jax.ShapeDtypeStruct((total, width), bf16)] * 3,
            jax.ShapeDtypeStruct((gates_of, total), f32),
        ],
        [pltpu.VMEM((span + 8, width), f32)],
        cost(6e9, 12 * total * width, total * width),
        "front",
        mixer, mixer, conv_taps, conv_shift, maps, gate_rows,
    )


def gates_kernel(span, share, head_ref, *refs):
    parts, bias_ref, out_ref = refs[:-2], refs[-2], refs[-1]
    pre = parts[0][...]
    for p in parts[1:]:
        pre = pre + p[...]
    if share != 1.0:
        pre = pre * share
    pre = pre + bias_ref[...]
    rows, total = pre.shape
    head = head_ref[0]
    at = lax.broadcasted_iota(jnp.int32, pre.shape, 0)
    lane = lax.broadcasted_iota(jnp.int32, (8, total), 1)
    in_gate = jnp.sum(jnp.where(at == head, pre, 0.0), axis=0, keepdims=True)
    forget = jnp.sum(jnp.where(at == head + rows // 2, pre, 0.0), axis=0, keepdims=True)
    forget = jnp.broadcast_to(forget, (8, total))
    log_forget = jnp.minimum(forget, 0.0) - jnp.log1p(jnp.exp(-jnp.abs(forget)))
    place = lane % span
    running = log_forget
    by = 1
    while by < span:
        running = running + jnp.where(place >= by, pltpu.roll(running, by, 1), 0.0)
        by *= 2
    whole_sum = jnp.where(place == span - 1, running, 0.0)
    by = 1
    while by < span:
        whole_sum = whole_sum + pltpu.roll(whole_sum, total - by, 1) * jnp.where(
            place < span - by, 1.0, 0.0
        )
        by *= 2
    out_ref[0:1, :] = in_gate
    out_ref[1:2, :] = running[0:1]
    out_ref[2:3, :] = whole_sum[0:1]
    out_ref[3:4, :] = jax.nn.sigmoid(-forget)[0:1]
    out_ref[4:8, :] = jnp.zeros((4, total), f32)


def gates(head, parts, bias, span, share):
    rows, total = parts[0].shape
    full = pl.BlockSpec((rows, total), lambda i, s: (0, 0))
    return pl.pallas_call(
        partial(gates_kernel, span, share),
        grid_spec=pltpu.PrefetchScalarGridSpec(
            num_scalar_prefetch=1,
            grid=(1,),
            in_specs=[full] * len(parts) + [pl.BlockSpec((rows, 1), lambda i, s: (0, 0))],
            out_specs=pl.BlockSpec((8, total), lambda i, s: (0, 0)),
        ),
        out_shape=jax.ShapeDtypeStruct((8, total), f32),
        name="gates",
    )(head.reshape(1).astype(jnp.int32), *parts, bias)


def column_of(row):
    n = row.shape[1]
    eye = lax.broadcasted_iota(jnp.int32, (n, n), 0) == lax.broadcasted_iota(jnp.int32, (n, n), 1)
    return jnp.sum(jnp.where(eye, jnp.broadcast_to(row, (n, n)), 0.0), axis=1, keepdims=True)


def row_of(column):
    n = column.shape[0]
    eye = lax.broadcasted_iota(jnp.int32, (n, n), 0) == lax.broadcasted_iota(jnp.int32, (n, n), 1)
    return jnp.sum(jnp.where(eye, jnp.broadcast_to(column, (n, n)), 0.0), axis=0, keepdims=True)


def tile_weights(gate_ref, column, reach, lanes, n, causal):
    row = gate_ref[0:1, lanes] - gate_ref[1:2, lanes] + reach
    exponent = column + row
    if not causal:
        return jnp.exp(exponent)
    keep = lax.broadcasted_iota(jnp.int32, (n, n), 0) >= lax.broadcasted_iota(jnp.int32, (n, n), 1)
    return jnp.where(keep, jnp.exp(jnp.where(keep, exponent, 0.0)), 0.0)


def cell_kernel(
    at_ref, gate_ref, q_ref, k_ref, v_ref, pre_ref, gin_ref, skip_ref, og_ref,
    mix_ref, num_ref, hid_ref,
):
    n, width = q_ref.shape
    tb = pl.program_id(0)
    here = pl.ds(pl.multiple_of(tb * n, n), n)
    column = column_of(gate_ref[1:2, here])

    def one(sb, reach, causal):
        lanes = pl.ds(pl.multiple_of(sb * n, n), n)
        w = tile_weights(gate_ref, column, reach, lanes, n, causal)
        mix = (w * dot_nt(q_ref[...], k_ref[lanes, :])).astype(bf16)
        mix_ref[:, lanes] = mix
        return dot_nn(mix, v_ref[lanes, :])

    num_ref[...] = one(tb, jnp.zeros((1, n), f32), True)

    def earlier(step, reach):
        sb = tb - 1 - step
        reach = reach + gate_ref[2:3, pl.ds(pl.multiple_of(sb * n, n), n)]
        num_ref[...] += one(sb, reach, False)
        return reach

    lax.fori_loop(0, tb, earlier, jnp.zeros((1, n), f32))
    skip, og = skip_ref[...], og_ref[...]

    def chunk(at):
        rows = pl.ds(at, 16)
        hat, _ = normalize(num_ref[rows, :])
        conv = silu_parts(pre_ref[rows, :])[1]
        act = silu_parts(gin_ref[rows, :])[1]
        hid_ref[rows, :] = ((hat * og + skip * conv) * act).astype(bf16)

    row_chunks(n, 16, chunk, 8)


def cell(place, gate, q, k, v, pre, gate_in, skip, out_gain, span):
    total, width = q.shape
    count = total // span

    def own(i, at):
        return (lax.rem(i + count - at[0], count), 0)

    tile = pl.BlockSpec((span, width), lambda i, at: (i, 0))
    moved = pl.BlockSpec((span, width), own)
    full = whole((total, width))
    return call(
        cell_kernel,
        place,
        count,
        [whole(gate.shape), tile, full, full, tile, moved, whole(skip.shape), whole(out_gain.shape)],
        [pl.BlockSpec((span, total), lambda i, at: (i, 0)), tile, moved],
        [
            jax.ShapeDtypeStruct((total, total), bf16),
            jax.ShapeDtypeStruct((total, width), f32),
            jax.ShapeDtypeStruct((total, width), bf16),
        ],
        [],
        cost(2.5 * total * width * total, 20 * total * width, 3 * total * width),
        "cell",
        gate, q, k, v, pre, gate_in, skip, out_gain,
    )


def tail_back_kernel(
    at_ref, bg_ref, num_ref, pre_ref, gin_ref, down_ref, skip_ref, og_ref,
    ng_ref, gg_ref, ct_ref, sums_ref, hg_ref,
):
    hg_ref[...] = dot_nt(bg_ref[...], down_ref[...])

    @pl.when(pl.program_id(0) == 0)
    def _():
        sums_ref[...] = jnp.zeros_like(sums_ref)

    skip, og = skip_ref[...], og_ref[...]

    def chunk(at):
        rows = pl.ds(at, 16)
        hat, scale = normalize(num_ref[rows, :])
        conv = silu_parts(pre_ref[rows, :])[1]
        before = hat * og + skip * conv
        gin = gin_ref[rows, :]
        sig, act = silu_parts(gin)
        hg = hg_ref[rows, :]
        gg_ref[rows, :] = (hg * before * (sig * (1.0 + gin * (1.0 - sig)))).astype(bf16)
        bgrad = hg * act
        sums_ref[0:8, :] += fold8(bgrad * conv)
        sums_ref[8:16, :] += fold8(bgrad * hat)
        ct_ref[rows, :] = bgrad * skip
        ng_ref[rows, :] = normalize_back(bgrad * og, hat, scale).astype(bf16)

    row_chunks(hg_ref.shape[0], 16, chunk, 8)


def tail_back(place, bg, num, pre, gate_in, w_down, skip, out_gain, span):
    model = bg.shape[1]
    total, width = num.shape
    count = total // span

    def own(i, at):
        return (lax.rem(i + count - at[0], count), 0)

    tile = pl.BlockSpec((span, width), lambda i, at: (i, 0))
    moved = pl.BlockSpec((span, width), own)
    return call(
        tail_back_kernel,
        place,
        count,
        [
            pl.BlockSpec((span, model), own), tile, tile, moved,
            whole(w_down.shape), whole(skip.shape), whole(out_gain.shape),
        ],
        [tile, moved, tile, pl.BlockSpec((16, width), lambda i, at: (0, 0))],
        [
            jax.ShapeDtypeStruct((total, width), bf16),
            jax.ShapeDtypeStruct((total, width), bf16),
            jax.ShapeDtypeStruct((total, width), f32),
            jax.ShapeDtypeStruct((16, width), f32),
        ],
        [pltpu.VMEM((span, width), f32)],
        cost(2 * total * model * width, 24 * total * width, 2 * total * width),
        "tail_back",
        bg, num, pre, gate_in, w_down, skip, out_gain,
    )


def cell_back_kernel(
    gate_ref, q_ref, k_ref, v_ref, mix_ref, ng_ref,
    dq_ref, dk_ref, dv_ref, gout_ref, sums_ref,
):
    n, width = q_ref.shape
    total = k_ref.shape[0]
    tb = pl.program_id(0)
    here = pl.ds(pl.multiple_of(tb * n, n), n)
    column = column_of(gate_ref[1:2, here])

    @pl.when(tb == 0)
    def _():
        sums_ref[...] = jnp.zeros_like(sums_ref)

    def one(sb, reach, causal):
        lanes = pl.ds(pl.multiple_of(sb * n, n), n)
        w = tile_weights(gate_ref, column, reach, lanes, n, causal)
        mix = mix_ref[:, lanes]
        ng = ng_ref[...]
        mix_grad = dot_nt(ng, v_ref[lanes, :])
        exponent_grad = mix_grad * mix.astype(f32)
        scores_grad = (w * mix_grad).astype(bf16)
        sums_ref[0:1, lanes] += jnp.sum(exponent_grad, axis=0, keepdims=True)
        return (
            jnp.sum(exponent_grad, axis=1, keepdims=True),
            dot_nn(scores_grad, k_ref[lanes, :]),
            dot_tn(scores_grad, q_ref[...]),
            dot_tn(mix, ng),
            lanes,
        )

    by_row, dq, dk, dv, lanes = one(tb, jnp.zeros((1, n), f32), True)
    dq_ref[...] = dq
    dk_ref[lanes, :] = dk
    dv_ref[lanes, :] = dv

    def earlier(step, carry):
        reach, by_row = carry
        sb = tb - 1 - step
        reach = reach + gate_ref[2:3, pl.ds(pl.multiple_of(sb * n, n), n)]
        more, dq, dk, dv, lanes = one(sb, reach, False)
        dq_ref[...] += dq
        dk_ref[lanes, :] += dk
        dv_ref[lanes, :] += dv
        return reach, by_row + more

    _, by_row = lax.fori_loop(0, tb, earlier, (jnp.zeros((1, n), f32), by_row))
    sums_ref[1:2, here] = row_of(by_row)

    @pl.when(tb == pl.num_programs(0) - 1)
    def _():
        by_source = sums_ref[0:1, :]
        lane = lax.broadcasted_iota(jnp.int32, (8, total), 1)
        running = jnp.broadcast_to(sums_ref[1:2, :] - by_source, (8, total))
        by = 1
        while by < total:
            running = running + jnp.where(
                lane < total - by, pltpu.roll(running, total - by, 1), 0.0
            )
            by *= 2
        gout_ref[0:1, :] = by_source
        gout_ref[1:2, :] = running[0:1] * gate_ref[3:4, :]


def cell_back(gate, q, k, v, mix, num_grad, span):
    total, width = q.shape
    tile = pl.BlockSpec((span, width), lambda i: (i, 0))
    full = whole((total, width))
    return pl.pallas_call(
        cell_back_kernel,
        grid=(total // span,),
        in_specs=[
            whole(gate.shape), tile, full, full,
            pl.BlockSpec((span, total), lambda i: (i, 0)), tile,
        ],
        out_specs=[
            tile,
            pl.BlockSpec((total, width), lambda i: (0, 0)),
            pl.BlockSpec((total, width), lambda i: (0, 0)),
            pl.BlockSpec((2, total), lambda i: (0, 0)),
        ],
        out_shape=[
            *[jax.ShapeDtypeStruct((total, width), f32)] * 3,
            jax.ShapeDtypeStruct((2, total), f32),
        ],
        scratch_shapes=[pltpu.VMEM((8, total), f32)],
        compiler_params=kernel_params(),
        cost_estimate=cost(
            5 * total * total * width, 24 * total * width, total * total
        ),
        name="cell_back",
    )(gate, q, k, v, mix, num_grad)


def back_kernel(
    key_scale, heads, at_ref, dq_ref, dk_ref, dv_ref, q_ref, k_ref, v_ref, pre_ref, mix_ref, ct_ref,
    taps_ref, maps_ref, gates_ref, *refs,
):
    gate_parts, sums_ref = refs[:heads], refs[heads]
    mg_ref, pack_ref, tg_ref, wg_ref, grow_ref, gsum_ref, gb_ref, pg_ref, mv_ref = refs[heads + 1 :]
    rows, width = dq_ref.shape
    taps = taps_ref.shape[0]
    lanes = maps_ref.shape[1]
    block = width // lanes
    per_map = block * block

    @pl.when(pl.program_id(0) == 0)
    def _():
        tg_ref[...] = jnp.zeros_like(tg_ref)
        wg_ref[...] = jnp.zeros_like(wg_ref)
        grow_ref[...] = jnp.zeros_like(grow_ref)
        gsum_ref[...] = jnp.zeros_like(gsum_ref)
        pg_ref[rows : rows + 8, :] = jnp.zeros((8, width), f32)

    gg = jnp.concatenate([p[...] for p in gate_parts], axis=0)
    gsum_ref[...] += jnp.broadcast_to(jnp.sum(gg, axis=1, keepdims=True), gsum_ref.shape)
    high = gg.astype(bf16)
    low = (gg - high.astype(f32)).astype(bf16)
    both = jnp.concatenate([high, low], axis=0)
    for m, x_ref in enumerate((q_ref, k_ref, v_ref)):
        gb_ref[m] = dot_tn(both, gates_ref[m])
        grow = dot_nn(both, x_ref[...])
        grow_ref[m] += grow[: 2 * heads] + grow[2 * heads :]

    size = 32

    def chunk(at):
        here = pl.ds(at, size)

        def cols(i):
            return slice(i * lanes, (i + 1) * lanes)

        def weight(m, i, o):
            r = (m * block + i) * block + o
            return maps_ref[r : r + 1, :]

        pre = [pre_ref[here, cols(i)] for i in range(block)]
        parts = [silu_parts(p) for p in pre]
        conv_grad = [ct_ref[here, cols(i)] for i in range(block)]
        for m, (g_ref, scale) in enumerate(((dq_ref, None), (dk_ref, key_scale))):
            for o in range(block):
                g = g_ref[here, cols(o)] + gb_ref[m, here, cols(o)]
                if scale is not None:
                    g = g * scale
                for i in range(block):
                    conv_grad[i] = conv_grad[i] + g * weight(m, i, o)
                    wg_ref[m * per_map + i * block + o] += fold8(parts[i][1] * g)
        for i in range(block):
            sig = parts[i][0]
            pg_ref[here, cols(i)] = conv_grad[i] * (sig * (1.0 + pre[i] * (1.0 - sig)))
        mixed = [mix_ref[here, cols(i)].astype(f32) for i in range(block)]
        grads = [None] * block
        for o in range(block):
            g = dv_ref[here, cols(o)] + gb_ref[2, here, cols(o)]
            for i in range(block):
                term = g * weight(2, i, o)
                grads[i] = term if grads[i] is None else grads[i] + term
                wg_ref[2 * per_map + i * block + o] += fold8(mixed[i] * g)
        for i in range(block):
            mv_ref[here, cols(i)] = grads[i]

    row_chunks(rows, size, chunk)

    def second(at):
        here = pl.ds(at, size)
        for i in range(block):
            cols = slice(i * lanes, (i + 1) * lanes)
            x = pg_ref[pl.ds(at, size + 8), cols]
            m = mix_ref[here, cols].astype(f32)
            grad = mv_ref[here, cols]
            for j in range(taps):
                lead = taps - 1 - j
                moved = x[lead : lead + size]
                grad = grad + taps_ref[j : j + 1, cols] * moved
                tg_ref[j, :, cols] += fold8(moved * m)
            tg_ref[taps, :, cols] += fold8(x[0:size])
            mg_ref[here, cols] = grad.astype(bf16)

    row_chunks(rows, size, second)
    pg_ref[rows : rows + 8, :] = pg_ref[0:8, :]

    @pl.when(pl.program_id(0) == pl.num_programs(0) - 1)
    def _():
        pack_ref[...] = jnp.zeros_like(pack_ref)
        at = 0
        for j in range(taps + 1):
            pack_ref[at : at + 1, :] = jnp.sum(tg_ref[j], axis=0, keepdims=True)
            at += 1
        for r in range(3 * block):
            for o in range(block):
                pack_ref[at : at + 1, o * lanes : (o + 1) * lanes] = jnp.sum(
                    wg_ref[r * block + o], axis=0, keepdims=True
                )
            at += 1
        for m in range(3):
            pack_ref[at : at + 2 * heads, :] = grow_ref[m]
            at += 2 * heads
        for j in range(2):
            pack_ref[at : at + 1, :] = jnp.sum(sums_ref[8 * j : 8 * j + 8], axis=0, keepdims=True)
            at += 1
        sums = gsum_ref[...]
        diagonal = lax.broadcasted_iota(jnp.int32, sums.shape, 0) == lax.broadcasted_iota(
            jnp.int32, sums.shape, 1
        )
        pack_ref[at : at + 1, 0:128] = jnp.sum(
            jnp.where(diagonal, sums, 0.0), axis=0, keepdims=True
        )


def back(
    place, dq, dk, dv, gate_parts, q, k, v, pre, mixer, conv_tail, conv_taps, maps, gate_rows,
    tail_sums, key_scale, span, pack_rows,
):
    total, width = dq.shape
    count = total // span
    taps = conv_taps.shape[0]
    lanes = maps.shape[1]
    heads = len(gate_parts)

    def own(i, at):
        return (lax.rem(2 * count - 1 - i - at[0], count), 0)

    tile = pl.BlockSpec((span, width), lambda i, at: (count - 1 - i, 0))
    moved = pl.BlockSpec((span, width), own)
    return call(
        partial(back_kernel, key_scale, heads),
        place,
        count,
        [
            tile, tile, tile, tile, tile, tile, tile, moved, tile,
            whole(conv_taps.shape), whole(maps.shape), whole(gate_rows.shape),
            *[pl.BlockSpec((2, span), lambda i, at: (0, count - 1 - i))] * heads,
            whole(tail_sums.shape),
        ],
        [moved, pl.BlockSpec((pack_rows, width), lambda i, at: (0, 0))],
        [
            jax.ShapeDtypeStruct((total, width), bf16),
            jax.ShapeDtypeStruct((pack_rows, width), f32),
        ],
        [
            pltpu.VMEM((taps + 1, 8, width), f32),
            pltpu.VMEM((maps.shape[0], 8, lanes), f32),
            pltpu.VMEM((3, 2 * heads, width), f32),
            pltpu.VMEM((2 * heads, 128), f32),
            pltpu.VMEM((3, span, width), f32),
            pltpu.VMEM((span + 8, width), f32),
            pltpu.VMEM((span, width), f32),
        ],
        cost(12e9, 30 * total * width, 2 * total * width),
        "back",
        dq, dk, dv, q, k, v, pre, mixer, conv_tail, conv_taps, maps, gate_rows, *gate_parts,
        tail_sums,
    )


def assemble_kernel(count, at_ref, *refs):
    out_ref = refs[-1]
    inputs = refs[:-1]
    step = pl.program_id(0)
    halves = len(inputs) // (2 * count - 1)
    for half in range(halves):
        own, others = inputs[half * (2 * count - 1)], inputs[half * (2 * count - 1) + 1 : (half + 1) * (2 * count - 1)]
        at = half * count

        @pl.when(step == at)
        def _(ref=own):
            out_ref[...] = ref[...].astype(out_ref.dtype)

        for r in range(1, count):
            ahead, behind = others[2 * (r - 1)], others[2 * (count - r - 1) + 1]

            @pl.when((step == at + r) & (at_ref[0] + r < count))
            def _(ref=ahead):
                out_ref[...] = ref[...].astype(out_ref.dtype)

            @pl.when((step == at + r) & (at_ref[0] + r >= count))
            def _(ref=behind):
                out_ref[...] = ref[...].astype(out_ref.dtype)


def flat(own, hops):
    return [own] + [x for pair in hops for x in pair]


def assemble_half_kernel(count, kept, at_ref, *refs):
    assemble_kernel(count, at_ref, *(refs[1:] if kept else refs))


def assemble_half(place, own, hops, copies, half, kept):
    rows, width = own.shape
    count = len(hops) + 1
    heads = count // copies

    def out_map(i, at):
        return (0, half * heads + lax.rem(i + at[0], count) // copies)

    parts = flat(own, hops)
    specs = [whole((rows, width))] * len(parts)
    aliases = {}
    if kept is not None:
        parts, specs = [kept] + parts, [pl.BlockSpec(memory_space=pl.ANY)] + specs
        aliases = {1: 0}
    return pl.pallas_call(
        partial(assemble_half_kernel, count, kept is not None),
        grid_spec=pltpu.PrefetchScalarGridSpec(
            num_scalar_prefetch=1,
            grid=(count,),
            in_specs=specs,
            out_specs=pl.BlockSpec((rows, width), out_map),
        ),
        out_shape=jax.ShapeDtypeStruct((rows, 2 * heads * width), f32),
        input_output_aliases=aliases,
        compiler_params=kernel_params(),
        cost_estimate=cost(0, 6 * count * rows * width),
        name="assemble_half",
    )(place, *parts)


def assemble_rows(place, own, hops):
    rows, width = own.shape
    count = len(hops) + 1
    parts = flat(own, hops)
    return call(
        partial(assemble_kernel, count),
        place,
        count,
        [whole((rows, width))] * len(parts),
        pl.BlockSpec((rows, width), lambda i, at: (lax.rem(i + at[0], count), 0)),
        jax.ShapeDtypeStruct((count * rows, width), f32),
        [],
        cost(0, 6 * count * rows * width),
        "assemble_rows",
        *parts,
    )


def mix_grads_kernel(x_ref, g_ref, pack_ref, out_ref):
    rows = x_ref.shape[1]
    out_ref[0, :rows, :] = dot_tn(x_ref[...], g_ref[...]).astype(bf16)
    pack = pack_ref[0]
    fill = jnp.zeros((out_ref.shape[1] - rows - pack.shape[0], pack.shape[1]), f32)
    out_ref[0, rows:, :] = jnp.concatenate([pack, fill], axis=0).astype(bf16)


def mix_grads(normed, mixer_grad, pack, dp):
    total, width = normed.shape
    cols = mixer_grad.shape[1]
    rows = width // dp
    pack = pack.reshape(dp, pack.shape[0] // dp, cols)
    extra = -(-(pack.shape[1] + 1) // 16) * 16
    return pl.pallas_call(
        mix_grads_kernel,
        grid=(dp,),
        in_specs=[
            pl.BlockSpec((total, rows), lambda i: (0, i)),
            whole(mixer_grad.shape),
            pl.BlockSpec((1,) + pack.shape[1:], lambda i: (i, 0, 0)),
        ],
        out_specs=pl.BlockSpec((1, rows + extra, cols), lambda i: (i, 0, 0)),
        out_shape=jax.ShapeDtypeStruct((dp, rows + extra, cols), bf16),
        compiler_params=kernel_params(),
        cost_estimate=cost(2 * total * width * cols, 2 * (total * width + 2 * width * cols)),
        name="mix_grads",
    )(normed, mixer_grad, pack)


def unpack_kernel(per, taps, heads, block, x_ref, gain_ref, norm_ref, convw_ref, convb_ref, maps_ref, gates_ref, bias_ref, skip_ref, og_ref):
    copies = x_ref.shape[0] // heads
    dp = x_ref.shape[1]
    width = x_ref.shape[3]
    lanes = width // block
    inner = heads * width
    rows = norm_ref.shape[1] // dp

    def row(h, r):
        return x_ref[h * copies, r // per, r % per : r % per + 1, :].astype(f32)

    for d in range(dp):
        total = x_ref[0, d, per : per + 1, 0:rows].astype(f32)
        for h in range(1, heads):
            total = total + x_ref[h * copies, d, per : per + 1, 0:rows].astype(f32)
        norm_ref[:, d * rows : (d + 1) * rows] = total / gain_ref[:, d * rows : (d + 1) * rows]
    for h in range(heads):
        cols = slice(h * width, (h + 1) * width)
        for j in range(taps):
            convw_ref[j : j + 1, cols] = row(h, j)
        convb_ref[:, cols] = row(h, taps)
        at = taps + 1
        for m in range(3):
            for i in range(block):
                values = row(h, at)
                for o in range(block):
                    maps_ref[m, h, i, o : o + 1, :] = values[:, o * lanes : (o + 1) * lanes]
                at += 1
        for m in range(3):
            for j in range(heads):
                for p in range(2):
                    g = p * heads + (h + j) % heads
                    start = m * inner + h * width
                    gates_ref[g : g + 1, start : start + width] = row(h, at)
                    at += 1
        skip_ref[:, cols] = row(h, at)
        og_ref[:, cols] = row(h, at + 1)
        if h == 0:
            bias_ref[...] = row(h, at + 2)[:, 0:128]


def unpack(small, gain, per, taps, heads, block):
    width = small.shape[3]
    inner = heads * width
    shapes = [
        gain.shape, (taps, inner), (1, inner), (3, heads, block, block, width // block),
        (2 * heads, 3 * inner), (1, 128), (1, inner), (1, inner),
    ]
    return pl.pallas_call(
        partial(unpack_kernel, per, taps, heads, block),
        grid=(1,),
        in_specs=[whole(small.shape), whole(gain.shape)],
        out_specs=[pl.BlockSpec(x, lambda i, n=len(x): (0,) * n) for x in shapes],
        out_shape=[jax.ShapeDtypeStruct(x, f32) for x in shapes],
        compiler_params=kernel_params(),
        name="unpack",
    )(small, gain)


def merge(place, own, hops):
    rows, width = own.shape
    count = len(hops) + 1
    parts = flat(own, hops)
    return call(
        partial(assemble_kernel, count),
        place,
        count,
        [whole((rows, width))] * len(parts),
        pl.BlockSpec((rows, width), lambda i, at: (i, 0)),
        jax.ShapeDtypeStruct((count * rows, width), own.dtype),
        [],
        cost(0, 4 * count * rows * width),
        "merge",
        *parts,
    )


def after(x, *others):
    if isinstance(x, list):
        return list(lax.optimization_barrier((*x, *others))[: len(x)])
    return lax.optimization_barrier((x, *others))[0]


def fence(*values):
    return lax.optimization_barrier(values)


def pass_on(pair, axis, s):
    n = lax.axis_size(axis)
    return (
        lax.ppermute(pair[0], axis, [(i, i - 1) for i in range(1, n - s + 1)]),
        lax.ppermute(pair[1], axis, [(i, i + 1) for i in range(s - 1, n - 1)]),
    )


def scatter_on(blocks, moving, axis, s):
    n = lax.axis_size(axis)
    ahead, behind = blocks[n - s], blocks[s]
    if s > 1:
        ahead = (ahead.astype(f32) + moving[0].astype(f32)).astype(bf16)
        behind = (behind.astype(f32) + moving[1].astype(f32)).astype(bf16)
    return (
        lax.ppermute(ahead, axis, [(i, i + 1) for i in range(s)]),
        lax.ppermute(behind, axis, [(i, i - 1) for i in range(n - s, n)]),
    )


def scatter_sum(own, terms):
    total = own.astype(f32)
    for term in terms:
        total = total + term.astype(f32)
    return total


def spread(x, axis, offsets):
    n = lax.axis_size(axis)
    return [
        x if r == 0 else lax.ppermute(x, axis, [(i, (i - r) % n) for i in range(n)]) for r in offsets
    ]


def on_device(
    inputs,
    lengths,
    norm_gain,
    up_weight,
    conv_weight,
    conv_bias,
    qkv_weight,
    gate_weight,
    gate_bias,
    skip_weight,
    outnorm_weight,
    down_weight,
    grad_out,
):
    span = inputs.shape[1]
    width = inputs.shape[2]
    inner = conv_weight.shape[1]
    taps = conv_weight.shape[0]
    heads = qkv_weight.shape[1]
    block = qkv_weight.shape[2]
    head_dim = inner // heads
    dp = lax.axis_size("dp")
    ctx = lax.axis_size("ctx")
    copies = ctx // heads
    total = ctx * span
    ctx_index = lax.axis_index("ctx")
    place = ctx_index.reshape(1).astype(jnp.int32)
    head = ctx_index // copies
    share = 1.0 / copies

    def columns_of(w, start):
        return lax.dynamic_slice_in_dim(w, start, head_dim, axis=w.ndim - 1)

    def by_offset(x):
        return [x[r * span : (r + 1) * span] for r in range(ctx)]

    live = (ctx_index * span + jnp.arange(span) < lengths[0]).astype(f32)[:, None]
    x_own = inputs[0].astype(f32)
    out_grad = grad_out[0].astype(f32) * live
    gain = norm_gain.astype(f32)[None]
    own_hat, own_scale = normalize(x_own)
    own_normed = (own_hat * gain).astype(bf16)
    own_mix = columns_of(up_weight, head * head_dim)
    own_gate = columns_of(up_weight, inner + head * head_dim)
    own_bg = out_grad.astype(bf16)
    unit = down_weight.shape[0] // ctx
    units = [
        ((h * dp + d) * copies + r, d * ctx + h * copies + r)
        for h in range(heads)
        for d in range(dp)
        for r in range(copies)
    ]
    w_mix = lax.all_gather(own_mix, "dp", axis=0, tiled=True)
    hops = [pass_on((own_normed, own_normed), "ctx", 1)]
    hops[0], own_normed, own_gate = fence(hops[0], own_normed, own_gate)
    w_gate = lax.all_gather(own_gate, "dp", axis=0, tiled=True)
    for s in range(2, ctx):
        hops.append(pass_on(hops[-1], "ctx", s))
        if s < ctx - 1:
            hops[-1], w_mix, down_weight = fence(hops[-1], w_mix, down_weight)
    w_down = lax.all_gather(down_weight, "dp", axis=0, tiled=True)
    hops, w_mix, own_bg = fence(hops, w_mix, own_bg)

    conv_taps = columns_of(conv_weight, head * head_dim).astype(f32)
    conv_shift = columns_of(conv_bias, head * head_dim).astype(f32)[None]
    skip = columns_of(skip_weight, head * head_dim).astype(f32)[None]
    out_gain = columns_of(outnorm_weight, head * head_dim).astype(f32)[None]
    maps = lax.dynamic_slice_in_dim(qkv_weight, head, 1, axis=1).astype(f32)
    maps = maps.reshape(3 * block * block, head_dim // block)
    gate_rows = columns_of(gate_weight.reshape(2 * heads, 3, inner), head * head_dim)
    gate_rows = gate_rows.transpose(1, 0, 2)
    turned = gate_rows.reshape(3, 2, heads, head_dim).transpose(0, 2, 1, 3)
    turned = jnp.concatenate([turned, turned], axis=1)
    turned = lax.dynamic_slice_in_dim(turned, head, heads, axis=1)
    turned = turned.reshape(3, 2 * heads, head_dim)
    turned = jnp.concatenate([turned, turned], axis=1)
    key_scale = head_dim ** (-0.5)
    pack_rows = -(-(taps + 4 + 3 * block + 6 * heads) // dp) * dp

    bg_hops = [pass_on((own_bg, own_bg), "ctx", 1)]
    normed = merge(place, own_normed, hops)
    mixer = dot_nn(normed, w_mix).astype(bf16)
    gate_in = dot_nn(normed, w_gate)
    bg_hops, normed, mixer, gate_in = fence(bg_hops, normed, mixer, gate_in)
    if ctx > 3:
        bg_hops.append(pass_on(bg_hops[-1], "ctx", 2))
    pre, queries, keys, values, gate_part = front(
        place, mixer, conv_taps, conv_shift, maps, gate_rows, key_scale, span
    )
    pre, gate_part = fence(pre, gate_part)
    gate_parts = spread(gate_part, "ctx", range(ctx))
    gate = gates(head, gate_parts, gate_bias.astype(f32)[:, None], span, share)
    bg_hops, gate = fence(bg_hops, gate)
    for s in range(len(bg_hops) + 1, ctx):
        bg_hops.append(pass_on(bg_hops[-1], "ctx", s))
    mix, num, hidden = cell(
        place, gate, queries, keys, values, pre, gate_in, skip, out_gain, span
    )
    w_down = lax.dynamic_slice_in_dim(w_down, head * head_dim, head_dim, axis=0)
    branch = (dot_nn(hidden, w_down) * share).astype(bf16)
    bg_hops, branch, hidden, w_down = fence(bg_hops, branch, hidden, w_down)
    branch_blocks = by_offset(branch)
    moving = scatter_on(branch_blocks, None, "ctx", 1)
    bg = merge(place, own_bg, bg_hops)
    down_grad = dot_tn(hidden, bg).astype(bf16)
    down_grad, bg = fence(down_grad, bg)
    down_part = lax.psum_scatter(down_grad, "dp", scatter_dimension=0, tiled=True)
    num_grad, gate_in_grad, conv_tail, tail_sums = tail_back(
        place, bg, num, pre, gate_in, w_down, skip, out_gain, span
    )
    num_grad, gate_in_grad, moving = fence(num_grad, gate_in_grad, moving)
    moving = scatter_on(branch_blocks, moving, "ctx", 2)
    up_gate = dot_tn(normed, gate_in_grad).astype(bf16)
    num_grad, up_gate, gate_in_grad = fence(num_grad, up_gate, gate_in_grad)
    gate_grad_part = lax.psum_scatter(up_gate, "dp", scatter_dimension=0, tiled=True)
    dq, dk, dv, gate_own = cell_back(gate, queries, keys, values, mix, num_grad, span)
    dq, gate_own, moving, gate_in_grad, down_part = fence(
        dq, gate_own, moving, gate_in_grad, down_part
    )
    gate_grads = spread(gate_own, "ctx", range(0, ctx, copies))
    gate_normed = dot_nt(gate_in_grad, w_gate)
    dq, gate_grads, moving, gate_normed = fence(dq, gate_grads, moving, gate_normed)
    for s in range(3, ctx):
        moving = scatter_on(branch_blocks, moving, "ctx", s)
    down_part = lax.dynamic_slice_in_dim(down_part, (ctx_index % copies) * unit, unit, axis=0)
    down_part = lax.ppermute(down_part, ("dp", "ctx"), [(b, a) for a, b in units])
    mixer_grad, pack = back(
        place, dq, dk, dv, gate_grads, queries, keys, values, pre, mixer, conv_tail,
        conv_taps, maps, turned, tail_sums, key_scale, span, pack_rows,
    )
    mixer_grad, moving, pack, down_part = fence(mixer_grad, moving, pack, down_part)
    down_hops = [pass_on((down_part, down_part), "ctx", 1)]
    up_mix = mix_grads(normed, mixer_grad, pack, dp)
    up_mix, mixer_grad, gate_grad_part = fence(up_mix, mixer_grad, gate_grad_part)
    mix_grad_part = lax.psum_scatter(up_mix, "dp", scatter_dimension=0, tiled=False)
    gate_hops = [pass_on((gate_grad_part, gate_grad_part), "ctx", 1)]
    normed_part = ((dot_nt(mixer_grad, w_mix) + gate_normed) * share).astype(bf16)
    normed_part, down_hops, gate_hops, moving = fence(normed_part, down_hops, gate_hops, moving)
    normed_blocks = by_offset(normed_part)
    outputs = (live * (x_own + scatter_sum(branch_blocks[0], moving))).astype(bf16)[None]
    moving = None
    mix_hops = []
    for s in range(1, ctx):
        moving = scatter_on(normed_blocks, moving, "ctx", s)
        for hops in (down_hops, gate_hops):
            if len(hops) < ctx - 1:
                hops.append(pass_on(hops[-1], "ctx", len(hops) + 1))
        if s > 1:
            have = mix_hops[-1] if mix_hops else (mix_grad_part, mix_grad_part)
            mix_hops.append(pass_on(have, "ctx", s - 1))
        if s == 1:
            moving, down_hops, gate_hops, outputs, mix_grad_part = fence(
                moving, down_hops, gate_hops, outputs, mix_grad_part
            )
            rows = width // dp
            per = pack_rows // dp
            small = mix_grad_part[rows : rows + 16]
            mix_grad_part = mix_grad_part[:rows]
            gain_part = mix_grad_part.astype(f32) * own_mix.astype(f32)
            gain_part = gain_part + gate_grad_part.astype(f32) * own_gate.astype(f32)
            gain_part = jnp.pad(jnp.sum(gain_part, axis=1)[None], ((0, 0), (0, head_dim - rows)))
            at = lax.broadcasted_iota(jnp.int32, (16, 1), 0)
            small = jnp.where(at == per, gain_part.astype(bf16), small)[: -(-(per + 1) // 8) * 8]
        elif s == 2:
            small = lax.all_gather(after(small, *gate_hops[-1]), "dp", axis=0)
            small = lax.all_gather(small, "ctx", axis=0)
            moving, down_hops, gate_hops, mix_hops, small = fence(
                moving, down_hops, gate_hops, mix_hops, small
            )
        else:
            moving, down_hops, gate_hops, mix_hops = fence(moving, down_hops, gate_hops, mix_hops)
    mix_hops.append(pass_on(mix_hops[-1], "ctx", ctx - 1))
    normed_grad = scatter_sum(normed_blocks[0], moving)
    input_grad = (out_grad + normalize_back(normed_grad * gain, own_hat, own_scale))[None]
    down_total = assemble_rows(place, down_part, down_hops)
    totals = unpack(small, gain, per, taps, heads, block)
    bias_total = totals[5][0, : 2 * heads].reshape(heads, 2).T.reshape(-1)
    up_total = assemble_half(place, gate_grad_part, gate_hops, copies, 1, None)
    up_total = assemble_half(place, mix_grad_part, mix_hops, copies, 0, up_total)
    return (
        outputs,
        input_grad,
        totals[0].reshape(-1),
        up_total,
        totals[1],
        totals[2].reshape(-1),
        totals[3],
        totals[4],
        bias_total,
        totals[6].reshape(-1),
        totals[7].reshape(-1),
        down_total,
    )


def solution(mesh):
    rows = P("dp", "ctx", None)
    weights = P("dp", None)
    return jax.shard_map(
        on_device,
        mesh=mesh,
        in_specs=(rows, P("dp"), P(), weights, *[P()] * 7, weights, rows),
        out_specs=(rows, rows, P(), weights, *[P()] * 7, weights),
        check_vma=False,
    )
```
